128 devices in a mesh: tm: 8 (over y_hi, x), freq: 16 (over z, y_lo, core).
Axes of the slice: x: 4, y: 4 (y_hi: 2, y_lo: 2; y = y_hi * 2 + y_lo), z: 4, core: 2. Of those that a mesh axis runs over, the one named last changes fastest.
Arguments:
- voltages: bfloat16 [512, 262144], P('freq', 'tm'), may hold values from -6 to 6
- station_flags: int32 [256], replicated, may hold values 0 or 1
- owner_map: int32 [1024], replicated, may hold values from 0 to 1023, each once
- beam_table: int32 [256], replicated, may hold values from 0 to 255, each once
- table_gains: float32 [256, 512], replicated, may hold values from 0.5 to 2
- table_delays: float32 [256, 512], replicated, may hold values from -8 to 8
Outputs:
- visibilities: bfloat16 [1024, 2, 512, 512], P(('tm', 'freq'))
- beam_voltages: bfloat16 [1024, 128, 2, 256], P(('tm', 'freq'))
The draws below stay inside these ranges and needn't reach their ends.
Inputs may be any that keep to these rules, and one draw needn't show every extreme that they name: `owner_map`: every channel appears in exactly one slot. `beam_table`: every weight table belongs to exactly one beam.
All inputs are finite; a program needn't handle non-finite values.
Results may differ from the reference program's by a relative error of at most 0.007.
Values may be sent and summed in bfloat16 or wider, within the bound.
No kernel may reach another device: no remote copies, remote signals or barrier semaphores. Data moves between devices by JAX's collectives and lax.ppermute only.
A program may use at most 512 MiB of HBM per device.

```python
import math
import jax
import jax.numpy as jnp
from jax import lax

STATIONS = 256
INPUTS = 512
CH = 1024
L = 2048
TAPS = 16
BEAMS = 256
NTAB = 256
TF = 128
SAMPLES = 262144


def plant(entries, rng, least, largest):
    longest = entries.shape.index(max(entries.shape))
    spots = []
    for shift in (0, 1):
        where = [jax.random.randint(jax.random.fold_in(rng, axis), (), 0, length) for axis, length in enumerate(entries.shape)]
        where[longest] = (where[longest] + shift) % entries.shape[longest]
        spots.append(tuple(where))
    return entries.at[spots[0]].set(least).at[spots[1]].set(largest)


def levels(key, shape, shards, smallest, largest):
    def one(position, parts):
        draws = jax.random.uniform(jax.random.fold_in(jax.random.fold_in(key, 6), position), (parts,), jnp.float32, smallest / len(shards), largest / len(shards))
        return jnp.repeat(jnp.exp(draws), shape[position] // parts).reshape((-1,) + (1,) * (len(shape) - position - 1))

    factor_of = one(*shards[0])
    for cut in shards[1:]:
        factor_of = factor_of * one(*cut)
    return factor_of


def bell_draw(rng, shape, deviation, reach, cuts=(), kind=jnp.bfloat16):
    values = deviation * jax.random.normal(rng, shape, jnp.float32)
    if cuts:
        values = values * levels(rng, shape, cuts, -0.22, 0.18)
    return jnp.clip(values, -reach, reach).astype(kind)


def setup_inputs(seed: int = 0) -> dict:
    arg_keys = jax.random.split(jax.random.key(seed), 7)
    return {
        "voltages": bell_draw(arg_keys[0], (INPUTS, SAMPLES), 1.0, 6.0, ((0, 16), (1, 8))),
        "station_flags": plant((jax.random.randint(arg_keys[1], (STATIONS,), 0, 8) < 7).astype(jnp.int32), jax.random.fold_in(arg_keys[1], 1), 0, 1),
        "owner_map": jax.random.permutation(arg_keys[2], CH).astype(jnp.int32),
        "beam_table": jax.random.permutation(arg_keys[3], BEAMS).astype(jnp.int32),
        "table_gains": jnp.clip(jnp.exp(jax.random.uniform(arg_keys[4], (NTAB, INPUTS), jnp.float32, math.log(0.5), math.log(2.0))), 0.5, 2.0),
        "table_delays": jnp.clip(jax.random.uniform(arg_keys[5], (NTAB, INPUTS), jnp.float32, -8.0, 8.0), -8.0, 8.0),
    }


def taps_table():
    index = jnp.arange(TAPS * L).astype(jnp.float32)
    offset = (index - TAPS * L / 2 + 0.5) / L
    window = 0.5 - 0.5 * jnp.cos(2.0 * math.pi * (index + 0.5) / (TAPS * L))
    return (jnp.sinc(offset) * window).reshape(TAPS, L)

def dft_table():
    chan = jnp.arange(CH, dtype=jnp.int32)
    sample = jnp.arange(L, dtype=jnp.int32)
    product = chan[:, None] * sample[None, :] % L
    angle = product.astype(jnp.float32) * (2.0 * math.pi / L)
    return jnp.concatenate([jnp.cos(angle), -jnp.sin(angle)], 0).astype(jnp.bfloat16)

def beam_weights(chan_f, beam_table, table_gains, table_delays):
    select = (beam_table[:, None] == jnp.arange(NTAB, dtype=jnp.int32)[None, :]).astype(jnp.float32)
    gain = jnp.dot(select, table_gains, precision=lax.Precision.HIGHEST)
    delay = jnp.dot(select, table_delays, precision=lax.Precision.HIGHEST)
    angle = delay[None] * (chan_f[:, None, None] * (2.0 * math.pi / L))
    scale = 1.0 / math.sqrt(INPUTS)
    weight_re = (gain[None] * jnp.cos(angle) * scale).astype(jnp.bfloat16)
    weight_im = (-gain[None] * jnp.sin(angle) * scale).astype(jnp.bfloat16)
    upper = jnp.concatenate([weight_re, -weight_im], -1)
    lower = jnp.concatenate([weight_im, weight_re], -1)
    return jnp.concatenate([upper, lower], 1)

def reference(voltages, station_flags, owner_map, beam_table, table_gains, table_delays):
    taps = taps_table()
    history = jnp.zeros((INPUTS, (TAPS - 1) * L), jnp.bfloat16)
    extended = jnp.concatenate([history, voltages], 1).reshape(INPUTS, TF + TAPS - 1, L)
    total = jnp.zeros((INPUTS, TF, L), jnp.float32)
    for k in range(TAPS):
        total = total + taps[k][None, None, :] * extended[:, k:k + TF, :].astype(jnp.float32)
    filtered = total.astype(jnp.bfloat16)
    table = dft_table()
    spectra = jnp.einsum('kn,itn->kit', table.astype(jnp.float32), filtered.astype(jnp.float32))
    spectra = (spectra * (1.0 / math.sqrt(L))).astype(jnp.bfloat16).reshape(2, CH, INPUTS, TF)
    spectra = jnp.take(spectra, owner_map, axis=1)
    flag_mask = jnp.repeat(station_flags, 2).astype(jnp.bfloat16)
    slotted = spectra * flag_mask[None, None, :, None]
    slotted = jnp.transpose(slotted, (1, 0, 2, 3)).reshape(CH, 2 * INPUTS, TF)
    chan_all = owner_map.astype(jnp.float32)

    def one_slot(args):
        stacked, chan_f = args
        dense = stacked.astype(jnp.float32)
        gram = jnp.dot(dense, dense.T)
        inv = 1.0 / TF
        vis_re = (gram[:INPUTS, :INPUTS] + gram[INPUTS:, INPUTS:]) * inv
        vis_im = (gram[INPUTS:, :INPUTS] - gram[:INPUTS, INPUTS:]) * inv
        vis = jnp.stack([vis_re, vis_im], 0).astype(jnp.bfloat16)
        weights = beam_weights(chan_f[None], beam_table, table_gains, table_delays)[0]
        beams = jnp.dot(dense.T, weights.astype(jnp.float32).T)
        return (vis, beams.reshape(TF, 2, BEAMS).astype(jnp.bfloat16))
    visibilities, beam_voltages = lax.map(one_slot, (slotted, chan_all))
    return (visibilities, beam_voltages)
```

```python
import functools
import math

import jax
import jax.numpy as jnp
import numpy as np
from jax import lax
from jax.experimental import pallas as pl
from jax.experimental.pallas import tpu as pltpu
from jax.sharding import PartitionSpec as P

INPUTS = 512
CH = 1024
L = 2048
TAPS = 16
BEAMS = 256
NTAB = 256
PREV = 7
NEXT = 8
FR = 16
IN_DEV = 32
BF = jnp.bfloat16
F32 = jnp.float32
MIB = 1 << 20


def fit(fn, degree):
    nodes = np.cos(np.pi * (np.arange(64) + 0.5) / 64) * 0.125 + 0.125
    poly = np.polynomial.Chebyshev.fit(nodes, fn(np.sqrt(nodes)), degree, domain=[0.0, 0.25])
    return [float(c) for c in poly.convert(kind=np.polynomial.Polynomial).coef]


COS = fit(lambda r: np.cos(2 * np.pi * r), 7)
SIN = fit(lambda r: np.sin(2 * np.pi * r) / r, 7)


def horner(coefs, z):
    total = jnp.full_like(z, coefs[-1])
    for c in coefs[-2::-1]:
        total = total * z + c
    return total


def cos_sin_turns(turns):
    r = turns - jnp.floor(turns + 0.5)
    z = r * r
    return horner(COS, z), horner(SIN, z) * r


def taps_table():
    index = np.arange(TAPS * L).astype(np.float64)
    offset = (index - TAPS * L / 2 + 0.5) / L
    window = 0.5 - 0.5 * np.cos(2.0 * np.pi * (index + 0.5) / (TAPS * L))
    return (np.sinc(offset) * window).reshape(TAPS, L).astype(np.float32)


def row_order():
    m = np.zeros((128, 128), np.float32)
    for tm in range(8):
        for sr in range(4):
            for th in range(4):
                m[sr * 32 + tm * 4 + th, tm * 16 + sr * 4 + th] = 1
    return m


def lane_order():
    m = np.zeros((512, 512), np.float32)
    for fl in range(4):
        for tl in range(4):
            for i in range(32):
                m[fl * 128 + tl * 32 + i, tl * 128 + fl * 32 + i] = 1
    return m


def frame_order():
    m = np.zeros((128, 128), np.float32)
    for tl in range(4):
        for tm in range(8):
            for th in range(4):
                m[(tm * 16 + 8 + th * 4 + tl) % 128, tl * 32 + tm * 4 + th] = 1
    return m


def table_kernel(chan_ref, cos_ref, sin_ref):
    rows = chan_ref.shape[0]

    def group(g, carry):
        at = pl.ds(pl.multiple_of(g * 16, 16), 16)
        chan = chan_ref[at, :]
        n2 = lax.broadcasted_iota(jnp.int32, (16, 128), 1).astype(F32)
        c, s = cos_sin_turns(chan * n2 * (1.0 / L))
        a, b = cos_sin_turns(chan * (128.0 / L))
        for n1 in range(L // 128):
            cos_ref[at, n1 * 128 : (n1 + 1) * 128] = c.astype(BF)
            sin_ref[at, n1 * 128 : (n1 + 1) * 128] = (-s).astype(BF)
            if n1 < L // 128 - 1:
                c, s = c * a - s * b, s * a + c * b
        return carry

    lax.fori_loop(0, rows // 16, group, 0)


def make_table(chan):
    rows = 256
    spec = pl.BlockSpec((rows, L), lambda i: (i, 0))
    return pl.pallas_call(
        table_kernel,
        grid=(CH // rows,),
        in_specs=[pl.BlockSpec((rows, 128), lambda i: (i, 0))],
        out_specs=[spec, spec],
        out_shape=[jax.ShapeDtypeStruct((CH, L), BF)] * 2,
        cost_estimate=pl.CostEstimate(flops=16 * CH * L, transcendentals=0, bytes_accessed=8 * MIB),
        name="table",
    )(jnp.broadcast_to(chan[:, None], (CH, 128)))


def weight_kernel(chan_ref, gain_ref, delay_ref, out_ref):
    chan = chan_ref[pl.program_id(0)] * (1.0 / L)

    def group(g, carry):
        at = pl.ds(pl.multiple_of(g * 16, 16), 16)
        c, s = cos_sin_turns(delay_ref[at, :] * chan)
        gain = gain_ref[at, :] * (1.0 / math.sqrt(INPUTS))
        out_ref[0, 0, at, :] = (gain * c).astype(BF)
        out_ref[0, 1, at, :] = (-(gain * s)).astype(BF)
        return carry

    lax.fori_loop(0, INPUTS // 16, group, 0)


def make_weights(chan_f, gain, delay):
    slots = chan_f.shape[0]
    whole = pl.BlockSpec((INPUTS, BEAMS), lambda i: (0, 0))
    return pl.pallas_call(
        weight_kernel,
        grid=(slots,),
        in_specs=[pl.BlockSpec(memory_space=pltpu.SMEM), whole, whole],
        out_specs=pl.BlockSpec((1, 2, INPUTS, BEAMS), lambda i: (i, 0, 0, 0)),
        out_shape=jax.ShapeDtypeStruct((slots, 2, INPUTS, BEAMS), BF),
        cost_estimate=pl.CostEstimate(flops=50 * slots * INPUTS * BEAMS, transcendentals=0, bytes_accessed=6 * MIB),
        name="weights",
    )(chan_f, gain, delay)


def dft_kernel(keep_ref, prev_ref, own_ref, next_ref, taps_ref, cos_ref, sin_ref, out_ref, filt, stage):
    @pl.when(pl.program_id(0) == 0)
    def _():
        keep = keep_ref[0]

        def column(j, carry):
            at = pl.multiple_of(j * 128, 128)
            taps = [taps_ref[k : k + 1, pl.ds(at, 128)] for k in range(TAPS)]
            for g in range(IN_DEV // 16):
                rows = pl.ds(g * 16, 16)
                acc = [None] * FR
                for f in range(FR + TAPS - 1):
                    if f < PREV:
                        x = prev_ref[rows, pl.ds(f * L + at, 128)]
                    elif f < PREV + FR:
                        x = own_ref[rows, pl.ds((f - PREV) * L + at, 128)]
                    else:
                        x = next_ref[rows, pl.ds((f - PREV - FR) * L + at, 128)]
                    x = x.astype(F32)
                    if f == PREV + FR:
                        for o in range(FR - NEXT, FR):
                            acc[o] = acc[o] * keep
                    for o in range(max(0, f - TAPS + 1), min(FR - 1, f) + 1):
                        term = taps[f - o] * x
                        acc[o] = term if acc[o] is None else acc[o] + term
                    if f >= TAPS - 1:
                        o = f - TAPS + 1
                        filt[o * IN_DEV + g * 16 : o * IN_DEV + g * 16 + 16, pl.ds(at, 128)] = acc[o].astype(BF)
            return carry

        lax.fori_loop(0, L // 128, column, 0)

    rows = cos_ref.shape[0]
    for r, ref in enumerate((cos_ref, sin_ref)):
        acc = lax.dot_general(ref[...], filt[...], (((1,), (1,)), ((), ())), preferred_element_type=F32)
        acc = acc * (1.0 / math.sqrt(L))
        for th in range(4):
            stage[pl.ds(r * 4 + th, rows, stride=8), :] = acc[:, th * 128 : (th + 1) * 128]
    out_ref[...] = stage[...].astype(BF).reshape(out_ref.shape)


def make_spectra(keep, prev, own, nxt, cos, sin):
    rows = 256
    whole = lambda a: pl.BlockSpec(a.shape, lambda i: (0, 0), pipeline_mode=pl.Buffered(1))
    taps = jnp.asarray(taps_table())
    table = pl.BlockSpec((rows, L), lambda i: (i, 0))
    return pl.pallas_call(
        dft_kernel,
        grid=(CH // rows,),
        in_specs=[pl.BlockSpec(memory_space=pltpu.SMEM), whole(prev), whole(own), whole(nxt), whole(taps), table, table],
        out_specs=pl.BlockSpec((rows // 8, 64, 128), lambda i: (i, 0, 0)),
        out_shape=jax.ShapeDtypeStruct((128, 64, 128), BF),
        scratch_shapes=[pltpu.VMEM((FR * IN_DEV, L), BF), pltpu.VMEM((rows * 8, 128), F32)],
        compiler_params=pltpu.CompilerParams(vmem_limit_bytes=48 * MIB),
        cost_estimate=pl.CostEstimate(flops=4 * CH * L * 512, transcendentals=0, bytes_accessed=14 * MIB),
        name="spectra",
    )(keep, prev, own, nxt, taps, cos, sin)


def pair_kernel(flag_ref, rows_ref, lanes_ref, frames_ref, got_ref, weight_ref, vis_ref, beam_ref, z):
    for fh in range(4):
        parts = [got_ref[(fh * 4 + fl) * 8 : (fh * 4 + fl) * 8 + 8].reshape(128, 128) for fl in range(4)]
        block = jnp.concatenate(parts, 1)
        block = jnp.dot(rows_ref[...], block, preferred_element_type=F32).astype(BF)
        block = jnp.dot(block, lanes_ref[...], preferred_element_type=F32)
        flag = flag_ref[:, fh * 128 : (fh + 1) * 128]
        for tl in range(4):
            piece = (block[:, tl * 128 : (tl + 1) * 128] * flag).astype(BF)
            for s in range(2):
                for r in range(2):
                    at = (s * 2 + r) * 32
                    z[s, r * 128 + tl * 32 : r * 128 + tl * 32 + 32, fh * 128 : (fh + 1) * 128] = piece[at : at + 32]
    for s in range(2):
        w = z[s]
        wt = w.T
        re_t, im_t = wt[:, :128], wt[:, 128:]
        vt = jnp.concatenate([im_t, -re_t], 1)
        vis_ref[s, 0] = (jnp.dot(wt, w, preferred_element_type=F32) * (1.0 / 128)).astype(BF)
        vis_ref[s, 1] = (jnp.dot(vt, w, preferred_element_type=F32) * (1.0 / 128)).astype(BF)
        re, im = w[:128], w[128:]
        w_re, w_im = weight_ref[s, 0], weight_ref[s, 1]
        dot = functools.partial(jnp.dot, preferred_element_type=F32)
        b_re = (dot(re, w_re) + dot(-im, w_im)).astype(BF)
        b_im = (dot(re, w_im) + dot(im, w_re)).astype(BF)
        beams = dot(frames_ref[...], jnp.concatenate([b_re, b_im], 1))
        beam_ref[s] = beams.astype(BF)


def make_outputs(flags, got, weights):
    slots = weights.shape[0]
    consts = [jnp.asarray(m, BF) for m in (row_order(), lane_order(), frame_order())]
    whole = lambda a: pl.BlockSpec(a.shape, lambda i: (0, 0), pipeline_mode=pl.Buffered(1))
    return pl.pallas_call(
        pair_kernel,
        grid=(slots // 2,),
        in_specs=[whole(flags)]
        + [whole(m) for m in consts]
        + [
            pl.BlockSpec((128, 16, 128), lambda i: (0, i, 0)),
            pl.BlockSpec((2, 2, INPUTS, BEAMS), lambda i: (i, 0, 0, 0)),
        ],
        out_specs=[
            pl.BlockSpec((2, 2, INPUTS, INPUTS), lambda i: (i, 0, 0, 0)),
            pl.BlockSpec((2, 128, 2 * BEAMS), lambda i: (i, 0, 0)),
        ],
        out_shape=[
            jax.ShapeDtypeStruct((slots, 2, INPUTS, INPUTS), BF),
            jax.ShapeDtypeStruct((slots, 128, 2 * BEAMS), BF),
        ],
        scratch_shapes=[pltpu.VMEM((2, 256, INPUTS), BF)],
        compiler_params=pltpu.CompilerParams(vmem_limit_bytes=48 * MIB),
        cost_estimate=pl.CostEstimate(flops=5_000_000_000, transcendentals=0, bytes_accessed=16 * MIB),
        name="pairs",
    )(flags, *consts, got, weights)


def shards(voltages, station_flags, owner_map, beam_table, table_gains, table_delays):
    n_time = lax.axis_size("tm")
    n_freq = lax.axis_size("freq")
    per_dev = CH // (n_time * n_freq)
    tm = lax.axis_index("tm")
    prev = lax.ppermute(voltages[:, (FR - PREV) * L :], "tm", [(i, i + 1) for i in range(n_time - 1)])
    nxt = lax.ppermute(voltages[:, : NEXT * L], "tm", [(i, (i - 1) % n_time) for i in range(n_time)])
    order = owner_map.reshape(n_time, n_freq, per_dev).transpose(1, 0, 2).reshape(CH)
    cos, sin = make_table(order.astype(F32))
    select = (beam_table[:, None] == jnp.arange(NTAB, dtype=jnp.int32)[None, :]).astype(F32)
    pick = lambda t: lax.dot_general(t, select, (((0,), (1,)), ((), ())), precision=lax.Precision.HIGHEST)
    start = (tm * n_freq + lax.axis_index("freq")) * per_dev
    chan_f = lax.dynamic_slice_in_dim(owner_map, start, per_dev).astype(F32)
    weights = make_weights(chan_f, pick(table_gains), pick(table_delays))
    keep = (tm != n_time - 1).astype(F32).reshape(1)
    spectra = make_spectra(keep, prev, voltages, nxt, cos, sin)
    got = lax.all_to_all(spectra, ("freq", "tm"), split_axis=0, concat_axis=0, tiled=True)
    flags = jnp.repeat(station_flags, 2).astype(F32).reshape(1, INPUTS)
    visibilities, beams = make_outputs(flags, got, weights)
    return (visibilities, beams.reshape(per_dev, 128, 2, BEAMS))


def solution(mesh):
    in_specs = (P("freq", "tm"), P(), P(), P(), P(), P())
    out_specs = (P(("tm", "freq"), None, None, None), P(("tm", "freq"), None, None, None))
    return jax.shard_map(shards, mesh=mesh, in_specs=in_specs, out_specs=out_specs, check_vma=False)
```

```python
import functools
import math

import jax
import jax.numpy as jnp
import numpy as np
from jax import lax
from jax.experimental import pallas as pl
from jax.experimental.pallas import tpu as pltpu
from jax.sharding import PartitionSpec as P

INPUTS = 512
CH = 1024
L = 2048
TAPS = 16
BEAMS = 256
NTAB = 256
FR = 16
IN_DEV = 32
SLOTS = 8
BF = jnp.bfloat16
F32 = jnp.float32
MIB = 1 << 20
VM = pl.BlockSpec(memory_space=pltpu.VMEM)
SM = pl.BlockSpec(memory_space=pltpu.SMEM)
ANY = pl.BlockSpec(memory_space=pl.ANY)


def fit(fn, degree):
    nodes = np.cos(np.pi * (np.arange(64) + 0.5) / 64) * 0.125 + 0.125
    poly = np.polynomial.Chebyshev.fit(nodes, fn(np.sqrt(nodes)), degree, domain=[0.0, 0.25])
    return [float(c) for c in poly.convert(kind=np.polynomial.Polynomial).coef]


COS = fit(lambda r: np.cos(2 * np.pi * r), 6)
NEG_SIN = fit(lambda r: -np.sin(2 * np.pi * r) / r, 6)


def horner(coefs, z):
    total = z * coefs[-1] + coefs[-2]
    for c in coefs[-3::-1]:
        total = total * z + c
    return total


def cos_negsin(turns):
    r = turns - jnp.floor(turns + 0.5)
    z = r * r
    return horner(COS, z), horner(NEG_SIN, z) * r


def taps_table():
    index = np.arange(TAPS * L).astype(np.float64)
    offset = (index - TAPS * L / 2 + 0.5) / L
    window = 0.5 - 0.5 * np.cos(2.0 * np.pi * (index + 0.5) / (TAPS * L))
    return (np.sinc(offset) * window).reshape(TAPS, L).astype(np.float32)


def lane_order():
    m = np.zeros((512, 512), np.float32)
    for fl in range(4):
        for tl in range(4):
            for i in range(32):
                m[fl * 128 + tl * 32 + i, tl * 128 + fl * 32 + i] = 1
    return m


def frames_of(phase):
    return [4 + u for u in range(8)] if phase == 0 else [0, 1, 2, 3, 12, 13, 14, 15]


def frame_order():
    m = np.zeros((256, 256), np.float32)
    for c in range(2):
        for tl in range(4):
            for tm in range(8):
                for ph in range(2):
                    for th in range(2):
                        o = frames_of(ph)[th * 4 + tl]
                        t = (tm * FR + 8 + o) % 128
                        m[t * 2 + c, c * 128 + tl * 32 + tm * 4 + ph * 2 + th] = 1
    return m


def table_kernel(chan_ref, cos_ref, sin_ref):
    def group(g, carry):
        chan = chan_ref[:, g].reshape(64, 128)
        n2 = lax.broadcasted_iota(jnp.int32, (64, 128), 1).astype(F32)
        c, s = cos_negsin(chan * n2 * (1.0 / L))
        a, b = cos_negsin(chan * (128.0 / L))
        at = pl.ds(pl.multiple_of(g * 64, 64), 64)
        for n1 in range(L // 128):
            cos_ref[at, n1 * 128 : (n1 + 1) * 128] = c.astype(BF)
            sin_ref[at, n1 * 128 : (n1 + 1) * 128] = s.astype(BF)
            if n1 < L // 128 - 1:
                c, s = c * a - s * b, s * a + c * b
        return carry

    lax.fori_loop(0, 16, group, 0)


def make_table(owner_map):
    chan = jnp.broadcast_to(owner_map.astype(F32)[:, None], (CH, 128)).reshape(8, 16, SLOTS, 128)
    return pl.pallas_call(
        table_kernel,
        in_specs=[VM],
        out_specs=[VM, VM],
        out_shape=[pltpu.VMEM((CH, L), BF)] * 2,
        cost_estimate=pl.CostEstimate(flops=16 * CH * L, transcendentals=0, bytes_accessed=8 * MIB),
        compiler_params=pltpu.CompilerParams(vmem_limit_bytes=4 * MIB),
        name="table",
    )(chan)


def weight_kernel(owner_ref, beam_ref, gains_ref, delays_ref, out_ref, gain, delay):
    def pick(g, carry):
        for j in range(8):
            b = g * 8 + j
            row = beam_ref[b]
            gain[pl.ds(b, 1), :] = gains_ref[pl.ds(row, 1), :]
            delay[pl.ds(b, 1), :] = delays_ref[pl.ds(row, 1), :]
        return carry

    lax.fori_loop(0, BEAMS // 8, pick, 0)
    start = (lax.axis_index("tm") * 16 + lax.axis_index("freq")) * SLOTS

    def group(g, carry):
        s = g // (BEAMS // 32)
        at = pl.ds(pl.multiple_of(g % (BEAMS // 32) * 32, 32), 32)
        chan = owner_ref[start + s].astype(F32) * (1.0 / L)
        c, n = cos_negsin(delay[at, :] * chan)
        scaled = gain[at, :] * (1.0 / math.sqrt(INPUTS))
        out_ref[s, 0, at, :] = (scaled * c).astype(BF)
        out_ref[s, 1, at, :] = (scaled * n).astype(BF)
        return carry

    lax.fori_loop(0, SLOTS * BEAMS // 32, group, 0)


def make_weights(owner_map, beam_table, gains, delays):
    return pl.pallas_call(
        weight_kernel,
        in_specs=[SM, SM, VM, VM],
        out_specs=VM,
        out_shape=pltpu.VMEM((SLOTS, 2, BEAMS, INPUTS), BF),
        scratch_shapes=[pltpu.VMEM((BEAMS, INPUTS), F32)] * 2,
        cost_estimate=pl.CostEstimate(flops=50 * SLOTS * INPUTS * BEAMS, transcendentals=0, bytes_accessed=6 * MIB),
        compiler_params=pltpu.CompilerParams(vmem_limit_bytes=4 * MIB),
        name="weights",
    )(owner_map, beam_table, gains, delays)


def spectra_kernel(phase, *refs):
    if phase == 0:
        own, p1, n1, taps_ref, cos_ref, sin_ref, out, filt, message, sem = refs
        p2 = n2 = None
    else:
        own, p1, n1, p2, n2, taps_ref, cos_ref, sin_ref, *_, out, filt, message, sem = refs
    pieces = [(p2, f) for f in range(4)] + [(p1, f) for f in range(3)] + [(own, f) for f in range(FR)]
    pieces += [(n1, f) for f in range(4)] + [(n2, f) for f in range(4)]
    outs = frames_of(phase)
    keep = (lax.axis_index("tm") != lax.axis_size("tm") - 1).astype(F32)

    def column(j, carry):
        at = pl.multiple_of(j * 128, 128)
        taps = [taps_ref[k : k + 1, pl.ds(at, 128)] for k in range(TAPS)]
        for g in range(IN_DEV // 16):
            acc = {}
            for f, (ref, i) in enumerate(pieces):
                hit = [o for o in outs if o <= f < o + TAPS]
                if f == 23:
                    for o in acc:
                        if o >= 8:
                            acc[o] = acc[o] * keep
                if not hit:
                    continue
                x = ref[g * 16 : g * 16 + 16, pl.ds(i * L + at, 128)].astype(F32)
                for o in hit:
                    term = taps[f - o] * x
                    acc[o] = acc[o] + term if o in acc else term
                if f - TAPS + 1 in acc:
                    o = f - TAPS + 1
                    u = outs.index(o) * IN_DEV + g * 16
                    filt[u : u + 16, pl.ds(at, 128)] = acc.pop(o).astype(BF)
        return carry

    lax.fori_loop(0, L // 128, column, 0)
    copies = []
    for q in range(4):
        rows = slice(q * 256, q * 256 + 256)
        dot = lambda ref: lax.dot_general(
            ref[rows, :], filt[...], (((1,), (1,)), ((), ())), preferred_element_type=F32
        ) * (1.0 / math.sqrt(L))
        re, im = dot(cos_ref), dot(sin_ref)
        for th in range(2):
            lanes = slice(th * 128, th * 128 + 128)
            both = [re[:, lanes].reshape(32, SLOTS, 128), im[:, lanes].reshape(32, SLOTS, 128)]
            message[q * 32 : q * 32 + 32, th * 16 : th * 16 + 16, :] = jnp.concatenate(both, 1).astype(BF)
        copy = pltpu.make_async_copy(
            message.at[pl.ds(q * 32, 32)], out.at[pl.ds(q * 32, 32), pl.ds(phase * 32, 32)], sem.at[q]
        )
        copy.start()
        copies.append(copy)
    for copy in copies:
        copy.wait()


def make_spectra(phase, parts, taps, cos, sin, after=(), before=None):
    args = [*parts, taps, cos, sin, *after] + ([] if before is None else [before])
    return pl.pallas_call(
        functools.partial(spectra_kernel, phase),
        in_specs=[VM] * (len(parts) + 3) + [ANY] * (len(args) - len(parts) - 3),
        out_specs=ANY,
        out_shape=jax.ShapeDtypeStruct((128, 64, 128), BF),
        input_output_aliases={} if before is None else {len(args) - 1: 0},
        scratch_shapes=[
            pltpu.VMEM((8 * IN_DEV, L), BF),
            pltpu.VMEM((128, 32, 128), BF),
            pltpu.SemaphoreType.DMA((4,)),
        ],
        cost_estimate=pl.CostEstimate(flops=4 * CH * L * 256, transcendentals=0, bytes_accessed=12 * MIB),
        compiler_params=pltpu.CompilerParams(vmem_limit_bytes=8 * MIB),
        name="spectra%d" % phase,
    )(*args)


def pair_kernel(flag_ref, lanes_ref, frames_ref, got_ref, weight_ref, vis, beam, y, vis_buf, beam_buf, sem, beam_sem):
    dot = functools.partial(jnp.dot, preferred_element_type=F32)
    dot_t = lambda a, b: lax.dot_general(a, b, (((1,), (1,)), ((), ())), preferred_element_type=F32)
    for fh in range(4):
        parts = [got_ref[(fh * 4 + fl) * 8 : (fh * 4 + fl) * 8 + 8].reshape(512, 128) for fl in range(4)]
        block = dot(jnp.concatenate(parts, 1), lanes_ref[...])
        flag = flag_ref[:, fh * 128 : (fh + 1) * 128]
        for tl in range(4):
            y[fh * 4 + tl] = block[:, tl * 128 : (tl + 1) * 128] * flag
    copies = {}
    for s in range(SLOTS):
        b = s % 2
        z = [
            jnp.concatenate(
                [
                    jnp.concatenate([y[fh * 4 + tl, pl.ds(r * 8 + s, 32, stride=16), :] for fh in range(4)], 1)
                    for tl in range(4)
                ],
                0,
            ).astype(BF)
            for r in range(2)
        ]
        w = jnp.concatenate(z, 0)
        wt = w.T
        vt = jnp.concatenate([wt[:, 128:], -wt[:, :128]], 1)
        if s >= 2:
            for copy in copies.pop(s - 2):
                copy.wait()
        started = []
        for c, left in enumerate((wt, vt)):
            vis_buf[b, c] = (dot(left, w) * (1.0 / 128)).astype(BF)
            started.append(pltpu.make_async_copy(vis_buf.at[b, c], vis.at[s, c], sem.at[b, c]))
            started[-1].start()
        w_re, w_im = weight_ref[s, 0], weight_ref[s, 1]
        b_re = dot_t(z[0], w_re) + dot_t(-z[1], w_im)
        b_im = dot_t(z[0], w_im) + dot_t(z[1], w_re)
        both = jnp.concatenate([b_re, b_im], 0).astype(BF)
        beam_buf[b] = dot(frames_ref[...], both).astype(BF).reshape(128, 2, BEAMS)
        started.append(pltpu.make_async_copy(beam_buf.at[b], beam.at[s], beam_sem.at[b]))
        started[-1].start()
        copies[s] = started
    for started in copies.values():
        for copy in started:
            copy.wait()


def make_outputs(flags, got, weights):
    consts = [jnp.asarray(m, BF) for m in (lane_order(), frame_order())]
    return pl.pallas_call(
        pair_kernel,
        in_specs=[VM] * 5,
        out_specs=[ANY, ANY],
        out_shape=[
            jax.ShapeDtypeStruct((SLOTS, 2, INPUTS, INPUTS), BF),
            jax.ShapeDtypeStruct((SLOTS, 128, 2, BEAMS), BF),
        ],
        scratch_shapes=[
            pltpu.VMEM((16, 512, 128), F32),
            pltpu.VMEM((2, 2, INPUTS, INPUTS), BF),
            pltpu.VMEM((2, 128, 2, BEAMS), BF),
            pltpu.SemaphoreType.DMA((2, 2)),
            pltpu.SemaphoreType.DMA((2,)),
        ],
        compiler_params=pltpu.CompilerParams(vmem_limit_bytes=16 * MIB),
        cost_estimate=pl.CostEstimate(flops=5_000_000_000, transcendentals=0, bytes_accessed=16 * MIB),
        name="pairs",
    )(flags, *consts, got, weights)


def shards(voltages, station_flags, owner_map, beam_table, table_gains, table_delays):
    n_time = lax.axis_size("tm")
    up = lambda a, b: lax.ppermute(voltages[:, a * L : b * L], "tm", [(i, i + 1) for i in range(n_time - 1)])
    down = lambda a, b: lax.ppermute(voltages[:, a * L : b * L], "tm", [(i, (i - 1) % n_time) for i in range(n_time)])
    p1, n1 = up(13, 16), down(0, 4)
    p2, n2 = up(9, 13), down(4, 8)
    cos, sin = make_table(owner_map)
    weights = make_weights(owner_map, beam_table, table_gains, table_delays)
    taps = jnp.asarray(taps_table())
    first = make_spectra(0, (voltages, p1, n1), taps, cos, sin)
    flags = jnp.repeat(station_flags, 2).astype(F32).reshape(1, INPUTS)
    spectra = make_spectra(1, (voltages, p1, n1, p2, n2), taps, cos, sin, (weights, flags), first)
    got = lax.all_to_all(spectra, ("freq", "tm"), split_axis=0, concat_axis=0, tiled=True)
    return make_outputs(flags, got, weights)


def solution(mesh):
    in_specs = (P("freq", "tm"), P(), P(), P(), P(), P())
    out_specs = (P(("tm", "freq"), None, None, None), P(("tm", "freq"), None, None, None))
    return jax.shard_map(shards, mesh=mesh, in_specs=in_specs, out_specs=out_specs, check_vma=False)
```

```python
import functools
import math

import jax
import jax.numpy as jnp
import numpy as np
from jax import lax
from jax.experimental import pallas as pl
from jax.experimental.pallas import tpu as pltpu
from jax.sharding import PartitionSpec as P

INPUTS = 512
CH = 1024
L = 2048
TAPS = 16
BEAMS = 256
NTAB = 256
FR = 16
IN_DEV = 32
SLOTS = 8
BF = jnp.bfloat16
F32 = jnp.float32
MIB = 1 << 20
VM = pl.BlockSpec(memory_space=pltpu.VMEM)
SM = pl.BlockSpec(memory_space=pltpu.SMEM)
ANY = pl.BlockSpec(memory_space=pl.ANY)
HB = pl.BlockSpec(memory_space=pltpu.HBM)


def fit(fn, degree):
    nodes = np.cos(np.pi * (np.arange(64) + 0.5) / 64) * 0.125 + 0.125
    poly = np.polynomial.Chebyshev.fit(nodes, fn(np.sqrt(nodes)), degree, domain=[0.0, 0.25])
    return [float(c) for c in poly.convert(kind=np.polynomial.Polynomial).coef]


COS = fit(lambda r: np.cos(2 * np.pi * r), 6)
NEG_SIN = fit(lambda r: -np.sin(2 * np.pi * r) / r, 6)


def horner(coefs, z):
    total = z * coefs[-1] + coefs[-2]
    for c in coefs[-3::-1]:
        total = total * z + c
    return total


def cos_negsin(turns):
    r = turns - jnp.floor(turns + 0.5)
    z = r * r
    return horner(COS, z), horner(NEG_SIN, z) * r


def taps_table():
    index = np.arange(TAPS * L).astype(np.float64)
    offset = (index - TAPS * L / 2 + 0.5) / L
    window = 0.5 - 0.5 * np.cos(2.0 * np.pi * (index + 0.5) / (TAPS * L))
    return (np.sinc(offset) * window).reshape(TAPS, L).astype(np.float32)


def lane_order():
    m = np.zeros((512, 512), np.float32)
    for fl in range(4):
        for tl in range(4):
            for i in range(32):
                m[fl * 128 + tl * 32 + i, tl * 128 + fl * 32 + i] = 1
    return m


def frames_of(phase):
    return [4 + u for u in range(8)] if phase == 0 else [0, 1, 2, 3, 12, 13, 14, 15]


def frame_order():
    m = np.zeros((256, 256), np.float32)
    for c in range(2):
        for tl in range(4):
            for tm in range(8):
                for ph in range(2):
                    for th in range(2):
                        o = frames_of(ph)[th * 4 + tl]
                        t = (tm * FR + 8 + o) % 128
                        m[t * 2 + c, c * 128 + tl * 32 + tm * 4 + ph * 2 + th] = 1
    return m


def table_kernel(chan_ref, cos_ref, sin_ref):
    def group(g, carry):
        chan = chan_ref[:, g].reshape(64, 128)
        n2 = lax.broadcasted_iota(jnp.int32, (64, 128), 1).astype(F32)
        c, s = cos_negsin(chan * n2 * (1.0 / L))
        a, b = cos_negsin(chan * (128.0 / L))
        at = pl.ds(pl.multiple_of(g * 64, 64), 64)
        for n1 in range(L // 128):
            cos_ref[at, n1 * 128 : (n1 + 1) * 128] = c.astype(BF)
            sin_ref[at, n1 * 128 : (n1 + 1) * 128] = s.astype(BF)
            if n1 < L // 128 - 1:
                c, s = c * a - s * b, s * a + c * b
        return carry

    lax.fori_loop(0, 16, group, 0)


def make_table(owner_map):
    chan = jnp.broadcast_to(owner_map.astype(F32)[:, None], (CH, 128)).reshape(8, 16, SLOTS, 128)
    return pl.pallas_call(
        table_kernel,
        in_specs=[VM],
        out_specs=[VM, VM],
        out_shape=[pltpu.VMEM((CH, L), BF)] * 2,
        cost_estimate=pl.CostEstimate(flops=16 * CH * L, transcendentals=0, bytes_accessed=8 * MIB),
        compiler_params=pltpu.CompilerParams(vmem_limit_bytes=4 * MIB),
        name="table",
    )(chan)


def weight_kernel(owner_ref, beam_ref, gains_ref, delays_ref, out_ref, gain, delay, made, sem):
    def pick(g, carry):
        for j in range(8):
            b = g * 8 + j
            row = beam_ref[b]
            gain[pl.ds(b, 1), :] = gains_ref[pl.ds(row, 1), :]
            delay[pl.ds(b, 1), :] = delays_ref[pl.ds(row, 1), :]
        return carry

    lax.fori_loop(0, BEAMS // 8, pick, 0)
    start = (lax.axis_index("tm") * 16 + lax.axis_index("freq")) * SLOTS

    copies = []
    for s in range(SLOTS):
        chan = owner_ref[start + s].astype(F32) * (1.0 / L)

        def group(g, carry):
            at = pl.ds(pl.multiple_of(g * 32, 32), 32)
            c, n = cos_negsin(delay[at, :] * chan)
            scaled = gain[at, :] * (1.0 / math.sqrt(INPUTS))
            made[s, 0, at, :] = (scaled * c).astype(BF)
            made[s, 1, at, :] = (scaled * n).astype(BF)
            return carry

        lax.fori_loop(0, BEAMS // 32, group, 0)
        copies.append(pltpu.make_async_copy(made.at[s], out_ref.at[s], sem.at[s]))
        copies[-1].start()
    for copy in copies:
        copy.wait()


def make_weights(owner_map, beam_table, gains, delays):
    return pl.pallas_call(
        weight_kernel,
        in_specs=[SM, SM, VM, VM],
        out_specs=HB,
        out_shape=pltpu.HBM((SLOTS, 2, BEAMS, INPUTS), BF),
        scratch_shapes=[
            pltpu.VMEM((BEAMS, INPUTS), F32),
            pltpu.VMEM((BEAMS, INPUTS), F32),
            pltpu.VMEM((SLOTS, 2, BEAMS, INPUTS), BF),
            pltpu.SemaphoreType.DMA((SLOTS,)),
        ],
        cost_estimate=pl.CostEstimate(flops=50 * SLOTS * INPUTS * BEAMS, transcendentals=0, bytes_accessed=6 * MIB),
        compiler_params=pltpu.CompilerParams(vmem_limit_bytes=8 * MIB),
        name="weights",
    )(owner_map, beam_table, gains, delays)


def cut_kernel(firsts, source, *refs):
    outs, sem = refs[:-1], refs[-1]
    copies = [
        pltpu.make_async_copy(source.at[:, pl.ds(first * L, out.shape[1])], out, sem.at[i])
        for i, (first, out) in enumerate(zip(firsts, outs))
    ]
    for copy in copies:
        copy.start()
    for copy in copies:
        copy.wait()


def cut(voltages, ranges, name):
    return pl.pallas_call(
        functools.partial(cut_kernel, [a for a, _ in ranges]),
        in_specs=[HB],
        out_specs=[ANY] * len(ranges),
        out_shape=[jax.ShapeDtypeStruct((IN_DEV, (b - a) * L), BF) for a, b in ranges],
        scratch_shapes=[pltpu.SemaphoreType.DMA((len(ranges),))],
        compiler_params=pltpu.CompilerParams(vmem_limit_bytes=MIB),
        cost_estimate=pl.CostEstimate(flops=0, transcendentals=0, bytes_accessed=2 * MIB),
        name=name,
    )(pltpu.with_memory_space_constraint(voltages, pltpu.HBM))


def spectra_kernel(phase, *refs):
    if phase == 0:
        own, p1, n1, taps_ref, cos_ref, sin_ref, out, held, filt, message, sem = refs
        p2 = n2 = None
    else:
        p2, n2, taps_ref, cos_ref, sin_ref, held, _, out, filt, message, sem = refs
        own = p1 = n1 = None
    pieces = [(p2, f) for f in range(4)] + [(p1, f) for f in range(3)] + [(own, f) for f in range(FR)]
    pieces += [(n1, f) for f in range(4)] + [(n2, f) for f in range(4)]
    now = frames_of(phase)
    later = frames_of(1)
    wanted = now + later if phase == 0 else now
    tm = lax.axis_index("tm")
    after_first = (tm != 0).astype(F32)
    before_last = (tm != lax.axis_size("tm") - 1).astype(F32)

    def column(j, carry):
        at = pl.multiple_of(j * 128, 128)
        lanes = pl.ds(at, 128)
        taps = [taps_ref[k : k + 1, lanes] for k in range(TAPS)]
        for g in range(IN_DEV // 16):
            rows = lambda o, among: slice(among.index(o) * IN_DEV + g * 16, among.index(o) * IN_DEV + g * 16 + 16)
            acc = {}
            for f, (ref, i) in enumerate(pieces):
                if f == 7:
                    for o in acc:
                        acc[o] = acc[o] * after_first
                    if phase == 1:
                        for o in now:
                            held_o = held[rows(o, later), lanes]
                            acc[o] = acc[o] + held_o if o in acc else held_o
                if f == 23 and phase == 0:
                    for o in acc:
                        if o >= 8:
                            acc[o] = acc[o] * before_last
                hit = [o for o in wanted if o <= f < o + TAPS]
                if ref is not None and hit:
                    x = ref[g * 16 : g * 16 + 16, pl.ds(i * L + at, 128)].astype(F32)
                    for o in hit:
                        term = taps[f - o] * x
                        acc[o] = acc[o] + term if o in acc else term
                for o in hit:
                    if o == f - TAPS + 1 and o in now:
                        filt[rows(o, now), lanes] = acc.pop(o).astype(BF)
                    elif o in later and phase == 0 and f == min(o + TAPS - 1, 26):
                        held[rows(o, later), lanes] = acc.pop(o)
        return carry

    lax.fori_loop(0, L // 128, column, 0)
    copies = []
    for q in range(4):
        rows = slice(q * 256, q * 256 + 256)
        dot = lambda ref: lax.dot_general(
            ref[rows, :], filt[...], (((1,), (1,)), ((), ())), preferred_element_type=F32
        ) * (1.0 / math.sqrt(L))
        re, im = dot(cos_ref), dot(sin_ref)
        for th in range(2):
            lanes = slice(th * 128, th * 128 + 128)
            both = [re[:, lanes].reshape(32, SLOTS, 128), im[:, lanes].reshape(32, SLOTS, 128)]
            message[q * 32 : q * 32 + 32, th * 16 : th * 16 + 16, :] = jnp.concatenate(both, 1).astype(BF)
        at = pl.ds(q * 32, 32)
        copies.append(pltpu.make_async_copy(message.at[at], out.at[at, pl.ds(phase * 32, 32)], sem.at[q]))
        copies[-1].start()
    for copy in copies:
        copy.wait()


def make_spectra(phase, args, before=None):
    args = [*args] + ([] if before is None else [before])
    out = pltpu.HBM((128, 64, 128), BF)
    return pl.pallas_call(
        functools.partial(spectra_kernel, phase),
        in_specs=[VM] * (len(args) - 1) + [HB if phase else VM],
        out_specs=HB if phase else [HB, VM],
        out_shape=out if phase else [out, pltpu.VMEM((8 * IN_DEV, L), F32)],
        input_output_aliases={len(args) - 1: 0} if phase else {},
        scratch_shapes=[
            pltpu.VMEM((8 * IN_DEV, L), BF),
            pltpu.VMEM((128, 32, 128), BF),
            pltpu.SemaphoreType.DMA((4,)),
        ],
        compiler_params=pltpu.CompilerParams(vmem_limit_bytes=8 * MIB),
        cost_estimate=pl.CostEstimate(flops=4 * CH * L * 256, transcendentals=0, bytes_accessed=12 * MIB),
        name="spectra%d" % phase,
    )(*args)


def pair_kernel(
    flag_ref, lanes_ref, frames_ref, got_ref, weights, vis, beam, y, vis_buf, beam_buf, weight_ref, sem, beam_sem, weight_sem
):
    dot = functools.partial(jnp.dot, preferred_element_type=F32)
    dot_t = lambda a, b: lax.dot_general(a, b, (((1,), (1,)), ((), ())), preferred_element_type=F32)
    fetches = [pltpu.make_async_copy(weights.at[s], weight_ref.at[s], weight_sem.at[s]) for s in range(SLOTS)]
    for fetch in fetches:
        fetch.start()
    for fh in range(4):
        parts = [got_ref[(fh * 4 + fl) * 8 : (fh * 4 + fl) * 8 + 8].reshape(512, 128) for fl in range(4)]
        block = dot(jnp.concatenate(parts, 1), lanes_ref[...])
        flag = flag_ref[:, fh * 128 : (fh + 1) * 128]
        for tl in range(4):
            y[fh * 4 + tl] = block[:, tl * 128 : (tl + 1) * 128] * flag
    copies = {}
    for s in range(SLOTS):
        b = s
        z = [
            jnp.concatenate(
                [
                    jnp.concatenate([y[fh * 4 + tl, pl.ds(r * 8 + s, 32, stride=16), :] for fh in range(4)], 1)
                    for tl in range(4)
                ],
                0,
            ).astype(BF)
            for r in range(2)
        ]
        w = jnp.concatenate(z, 0)
        wt = w.T
        vt = jnp.concatenate([wt[:, 128:], -wt[:, :128]], 1)
        started = []
        for c, left in enumerate((wt, vt)):
            vis_buf[b, c] = (dot(left, w) * (1.0 / 128)).astype(BF)
            started.append(pltpu.make_async_copy(vis_buf.at[b, c], vis.at[s, c], sem.at[b, c]))
            started[-1].start()
        fetches[s].wait()
        w_re, w_im = weight_ref[s, 0], weight_ref[s, 1]
        b_re = dot_t(z[0], w_re) + dot_t(-z[1], w_im)
        b_im = dot_t(z[0], w_im) + dot_t(z[1], w_re)
        both = jnp.concatenate([b_re, b_im], 0).astype(BF)
        beam_buf[b] = dot(frames_ref[...], both).astype(BF).reshape(128, 2, BEAMS)
        started.append(pltpu.make_async_copy(beam_buf.at[b], beam.at[s], beam_sem.at[b]))
        started[-1].start()
        copies[s] = started
    for started in copies.values():
        for copy in started:
            copy.wait()


def make_outputs(flags, got, weights):
    consts = [jnp.asarray(m, BF) for m in (lane_order(), frame_order())]
    return pl.pallas_call(
        pair_kernel,
        in_specs=[VM] * 4 + [HB],
        out_specs=[ANY, ANY],
        out_shape=[
            jax.ShapeDtypeStruct((SLOTS, 2, INPUTS, INPUTS), BF),
            jax.ShapeDtypeStruct((SLOTS, 128, 2, BEAMS), BF),
        ],
        scratch_shapes=[
            pltpu.VMEM((16, 512, 128), F32),
            pltpu.VMEM((SLOTS, 2, INPUTS, INPUTS), BF),
            pltpu.VMEM((SLOTS, 128, 2, BEAMS), BF),
            pltpu.VMEM((SLOTS, 2, BEAMS, INPUTS), BF),
            pltpu.SemaphoreType.DMA((SLOTS, 2)),
            pltpu.SemaphoreType.DMA((SLOTS,)),
            pltpu.SemaphoreType.DMA((SLOTS,)),
        ],
        compiler_params=pltpu.CompilerParams(vmem_limit_bytes=24 * MIB),
        cost_estimate=pl.CostEstimate(flops=5_000_000_000, transcendentals=0, bytes_accessed=16 * MIB),
        name="pairs",
    )(flags, *consts, got, pltpu.with_memory_space_constraint(weights, pltpu.HBM))


def shards(voltages, station_flags, owner_map, beam_table, table_gains, table_delays):
    n_time = lax.axis_size("tm")
    up = lambda x: lax.ppermute(x, "tm", [(i, (i + 1) % n_time) for i in range(n_time)])
    down = lambda x: lax.ppermute(x, "tm", [(i, (i - 1) % n_time) for i in range(n_time)])
    to_down, to_up = cut(voltages, [(0, 4), (13, 16)], "cut0")
    n1, p1 = down(to_down), up(to_up)
    to_down, to_up = cut(voltages, [(4, 8), (9, 13)], "cut1")
    n2, p2 = down(to_down), up(to_up)
    cos, sin = make_table(owner_map)
    taps = jnp.asarray(taps_table())
    first, held = make_spectra(0, (voltages, p1, n1, taps, cos, sin))
    spectra = make_spectra(1, (p2, n2, taps, cos, sin, held), first)
    weights = make_weights(owner_map, beam_table, table_gains, table_delays)
    flags = jnp.repeat(station_flags, 2).astype(F32).reshape(1, INPUTS)
    got = lax.all_to_all(spectra, ("freq", "tm"), split_axis=0, concat_axis=0, tiled=True)
    return make_outputs(flags, got, weights)


def solution(mesh):
    in_specs = (P("freq", "tm"), P(), P(), P(), P(), P())
    out_specs = (P(("tm", "freq"), None, None, None), P(("tm", "freq"), None, None, None))
    return jax.shard_map(shards, mesh=mesh, in_specs=in_specs, out_specs=out_specs, check_vma=False)
```

```python
import functools
import math

import jax
import jax.numpy as jnp
import numpy as np
from jax import lax
from jax.experimental import pallas as pl
from jax.experimental.pallas import tpu as pltpu
from jax.sharding import PartitionSpec as P

INPUTS = 512
CH = 1024
L = 2048
TAPS = 16
BEAMS = 256
NTAB = 256
FR = 16
IN_DEV = 32
SLOTS = 8
BF = jnp.bfloat16
F32 = jnp.float32
MIB = 1 << 20
VM = pl.BlockSpec(memory_space=pltpu.VMEM)
SM = pl.BlockSpec(memory_space=pltpu.SMEM)
ANY = pl.BlockSpec(memory_space=pl.ANY)
HB = pl.BlockSpec(memory_space=pltpu.HBM)


def fit(fn, degree):
    nodes = np.cos(np.pi * (np.arange(64) + 0.5) / 64) * 0.125 + 0.125
    poly = np.polynomial.Chebyshev.fit(nodes, fn(np.sqrt(nodes)), degree, domain=[0.0, 0.25])
    return [float(c) for c in poly.convert(kind=np.polynomial.Polynomial).coef]


COS = fit(lambda r: np.cos(2 * np.pi * r), 6)
NEG_SIN = fit(lambda r: -np.sin(2 * np.pi * r) / r, 6)


def horner(coefs, z):
    total = z * coefs[-1] + coefs[-2]
    for c in coefs[-3::-1]:
        total = total * z + c
    return total


def cos_negsin(turns):
    r = turns - jnp.floor(turns + 0.5)
    z = r * r
    return horner(COS, z), horner(NEG_SIN, z) * r


def taps_table():
    index = np.arange(TAPS * L).astype(np.float64)
    offset = (index - TAPS * L / 2 + 0.5) / L
    window = 0.5 - 0.5 * np.cos(2.0 * np.pi * (index + 0.5) / (TAPS * L))
    return (np.sinc(offset) * window).reshape(TAPS, L).astype(np.float32)


def lane_order():
    row = lax.broadcasted_iota(jnp.int32, (512, 512), 0)
    column = lax.broadcasted_iota(jnp.int32, (512, 512), 1)
    goal = ((row >> 5) & 3) * 128 + (row >> 7) * 32 + (row & 31)
    return (goal == column).astype(F32).astype(BF)


def frames_of(phase):
    return [4 + u for u in range(8)] if phase == 0 else [0, 1, 2, 3, 12, 13, 14, 15]


def frame_order():
    m = np.zeros((256, 256), np.float32)
    for c in range(2):
        for tl in range(4):
            for tm in range(8):
                for ph in range(2):
                    for th in range(2):
                        o = frames_of(ph)[th * 4 + tl]
                        t = (tm * FR + 8 + o) % 128
                        m[t * 2 + c, c * 128 + tl * 32 + tm * 4 + ph * 2 + th] = 1
    return m


def table_kernel(chan_ref, cos_ref, sin_ref):
    def group(g, carry):
        chan = chan_ref[:, g].reshape(64, 128)
        n2 = lax.broadcasted_iota(jnp.int32, (64, 128), 1).astype(F32)
        c, s = cos_negsin(chan * n2 * (1.0 / L))
        a, b = cos_negsin(chan * (128.0 / L))
        at = pl.ds(pl.multiple_of(g * 64, 64), 64)
        for n1 in range(L // 128):
            cos_ref[at, n1 * 128 : (n1 + 1) * 128] = c.astype(BF)
            sin_ref[at, n1 * 128 : (n1 + 1) * 128] = s.astype(BF)
            if n1 < L // 128 - 1:
                c, s = c * a - s * b, s * a + c * b
        return carry

    lax.fori_loop(0, 16, group, 0)


def make_table(owner_map):
    chan = jnp.broadcast_to(owner_map.astype(F32)[:, None], (CH, 128)).reshape(8, 16, SLOTS, 128)
    return pl.pallas_call(
        table_kernel,
        in_specs=[VM],
        out_specs=[VM, VM],
        out_shape=[pltpu.VMEM((CH, L), BF)] * 2,
        cost_estimate=pl.CostEstimate(flops=16 * CH * L, transcendentals=0, bytes_accessed=8 * MIB),
        compiler_params=pltpu.CompilerParams(vmem_limit_bytes=4 * MIB),
        name="table",
    )(chan)


def weight_kernel(owner_ref, beam_ref, gains_ref, delays_ref, out_ref, gain, delay, made, sem):
    def pick(g, carry):
        for j in range(8):
            b = g * 8 + j
            row = beam_ref[b]
            gain[pl.ds(b, 1), :] = gains_ref[pl.ds(row, 1), :]
            delay[pl.ds(b, 1), :] = delays_ref[pl.ds(row, 1), :]
        return carry

    lax.fori_loop(0, BEAMS // 8, pick, 0)
    start = (lax.axis_index("tm") * 16 + lax.axis_index("freq")) * SLOTS

    copies = []
    for s in range(SLOTS):
        chan = owner_ref[start + s].astype(F32) * (1.0 / L)

        def group(g, carry):
            at = pl.ds(pl.multiple_of(g * 32, 32), 32)
            c, n = cos_negsin(delay[at, :] * chan)
            scaled = gain[at, :] * (1.0 / math.sqrt(INPUTS))
            made[s, 0, at, :] = (scaled * c).astype(BF)
            made[s, 1, at, :] = (scaled * n).astype(BF)
            return carry

        lax.fori_loop(0, BEAMS // 32, group, 0)
        copies.append(pltpu.make_async_copy(made.at[s], out_ref.at[s], sem.at[s]))
        copies[-1].start()
    for copy in copies:
        copy.wait()


def make_weights(owner_map, beam_table, gains, delays):
    return pl.pallas_call(
        weight_kernel,
        in_specs=[SM, SM, VM, VM],
        out_specs=HB,
        out_shape=pltpu.HBM((SLOTS, 2, BEAMS, INPUTS), BF),
        scratch_shapes=[
            pltpu.VMEM((BEAMS, INPUTS), F32),
            pltpu.VMEM((BEAMS, INPUTS), F32),
            pltpu.VMEM((SLOTS, 2, BEAMS, INPUTS), BF),
            pltpu.SemaphoreType.DMA((SLOTS,)),
        ],
        cost_estimate=pl.CostEstimate(flops=50 * SLOTS * INPUTS * BEAMS, transcendentals=0, bytes_accessed=6 * MIB),
        compiler_params=pltpu.CompilerParams(vmem_limit_bytes=8 * MIB),
        name="weights",
    )(owner_map, beam_table, gains, delays)


def cut_kernel(firsts, source, *refs):
    outs, sem = refs[:-1], refs[-1]
    copies = [
        pltpu.make_async_copy(source.at[:, pl.ds(first * L, out.shape[1])], out, sem.at[i])
        for i, (first, out) in enumerate(zip(firsts, outs))
    ]
    for copy in copies:
        copy.start()
    for copy in copies:
        copy.wait()


def cut(voltages, ranges, name):
    return pl.pallas_call(
        functools.partial(cut_kernel, [a for a, _ in ranges]),
        in_specs=[HB],
        out_specs=[VM] * len(ranges),
        out_shape=[pltpu.VMEM((IN_DEV, (b - a) * L), BF) for a, b in ranges],
        scratch_shapes=[pltpu.SemaphoreType.DMA((len(ranges),))],
        compiler_params=pltpu.CompilerParams(vmem_limit_bytes=4 * MIB),
        cost_estimate=pl.CostEstimate(flops=0, transcendentals=0, bytes_accessed=2 * MIB),
        name=name,
    )(pltpu.with_memory_space_constraint(voltages, pltpu.HBM))


def spectra_kernel(phase, *refs):
    if phase == 0:
        own, p1, n1, taps_ref, cos_ref, sin_ref, out, held, filt, message, sem = refs
        p2 = n2 = None
    else:
        p2, n2, taps_ref, cos_ref, sin_ref, held, _, out, filt, message, sem = refs
        own = p1 = n1 = None
    pieces = [(p2, f) for f in range(4)] + [(p1, f) for f in range(3)] + [(own, f) for f in range(FR)]
    pieces += [(n1, f) for f in range(4)] + [(n2, f) for f in range(4)]
    now = frames_of(phase)
    later = frames_of(1)
    wanted = now + later if phase == 0 else now
    tm = lax.axis_index("tm")
    after_first = (tm != 0).astype(F32)
    before_last = (tm != lax.axis_size("tm") - 1).astype(F32)

    def column(j, carry):
        at = pl.multiple_of(j * 128, 128)
        lanes = pl.ds(at, 128)
        taps = [taps_ref[k : k + 1, lanes] for k in range(TAPS)]
        for g in range(IN_DEV // 16):
            rows = lambda o, among: slice(among.index(o) * IN_DEV + g * 16, among.index(o) * IN_DEV + g * 16 + 16)
            acc = {}
            for f, (ref, i) in enumerate(pieces):
                if f == 7:
                    for o in acc:
                        acc[o] = acc[o] * after_first
                    if phase == 1:
                        for o in now:
                            held_o = held[rows(o, later), lanes]
                            acc[o] = acc[o] + held_o if o in acc else held_o
                if f == 23 and phase == 0:
                    for o in acc:
                        if o >= 8:
                            acc[o] = acc[o] * before_last
                hit = [o for o in wanted if o <= f < o + TAPS]
                if ref is not None and hit:
                    x = ref[g * 16 : g * 16 + 16, pl.ds(i * L + at, 128)].astype(F32)
                    for o in hit:
                        term = taps[f - o] * x
                        acc[o] = acc[o] + term if o in acc else term
                for o in hit:
                    if o == f - TAPS + 1 and o in now:
                        filt[rows(o, now), lanes] = acc.pop(o).astype(BF)
                    elif o in later and phase == 0 and f == min(o + TAPS - 1, 26):
                        held[rows(o, later), lanes] = acc.pop(o)
        return carry

    lax.fori_loop(0, L // 128, column, 0)
    copies = []
    for q in range(4):
        rows = slice(q * 256, q * 256 + 256)
        dot = lambda ref: lax.dot_general(
            ref[rows, :], filt[...], (((1,), (1,)), ((), ())), preferred_element_type=F32
        ) * (1.0 / math.sqrt(L))
        re, im = dot(cos_ref), dot(sin_ref)
        for th in range(2):
            lanes = slice(th * 128, th * 128 + 128)
            both = [re[:, lanes].reshape(32, SLOTS, 128), im[:, lanes].reshape(32, SLOTS, 128)]
            message[q * 32 : q * 32 + 32, th * 16 : th * 16 + 16, :] = jnp.concatenate(both, 1).astype(BF)
        at = pl.ds(q * 32, 32)
        copies.append(pltpu.make_async_copy(message.at[at], out.at[at, pl.ds(phase * 32, 32)], sem.at[q]))
        copies[-1].start()
    for copy in copies:
        copy.wait()


def make_spectra(phase, args, before=None):
    args = [*args] + ([] if before is None else [before])
    out = pltpu.HBM((128, 64, 128), BF)
    return pl.pallas_call(
        functools.partial(spectra_kernel, phase),
        in_specs=[VM] * (len(args) - 1) + [HB if phase else VM],
        out_specs=HB if phase else [HB, VM],
        out_shape=out if phase else [out, pltpu.VMEM((8 * IN_DEV, L), F32)],
        input_output_aliases={len(args) - 1: 0} if phase else {},
        scratch_shapes=[
            pltpu.VMEM((8 * IN_DEV, L), BF),
            pltpu.VMEM((128, 32, 128), BF),
            pltpu.SemaphoreType.DMA((4,)),
        ],
        compiler_params=pltpu.CompilerParams(vmem_limit_bytes=8 * MIB),
        cost_estimate=pl.CostEstimate(flops=4 * CH * L * 256, transcendentals=0, bytes_accessed=12 * MIB),
        name="spectra%d" % phase,
    )(*args)


def pair_kernel(
    flag_ref, frames_ref, got_ref, weights, vis, beam, y, vis_buf, beam_buf, weight_ref, sem, beam_sem, weight_sem
):
    dot = functools.partial(jnp.dot, preferred_element_type=F32)
    dot_t = lambda a, b: lax.dot_general(a, b, (((1,), (1,)), ((), ())), preferred_element_type=F32)
    fetches = [pltpu.make_async_copy(weights.at[s], weight_ref.at[s], weight_sem.at[s]) for s in range(SLOTS)]
    for fetch in fetches:
        fetch.start()
    lanes = lane_order()
    for fh in range(4):
        parts = [got_ref[(fh * 4 + fl) * 8 : (fh * 4 + fl) * 8 + 8].reshape(512, 128) for fl in range(4)]
        block = dot(jnp.concatenate(parts, 1), lanes)
        flag = flag_ref[:, fh * 128 : (fh + 1) * 128]
        for tl in range(4):
            y[fh * 4 + tl] = block[:, tl * 128 : (tl + 1) * 128] * flag
    copies = {}
    for s in range(SLOTS):
        b = s
        z = [
            jnp.concatenate(
                [
                    jnp.concatenate([y[fh * 4 + tl, pl.ds(r * 8 + s, 32, stride=16), :] for fh in range(4)], 1)
                    for tl in range(4)
                ],
                0,
            ).astype(BF)
            for r in range(2)
        ]
        w = jnp.concatenate(z, 0)
        wt = w.T
        vt = jnp.concatenate([wt[:, 128:], -wt[:, :128]], 1)
        started = []
        for c, left in enumerate((wt, vt)):
            vis_buf[b, c] = (dot(left, w) * (1.0 / 128)).astype(BF)
            started.append(pltpu.make_async_copy(vis_buf.at[b, c], vis.at[s, c], sem.at[b, c]))
            started[-1].start()
        fetches[s].wait()
        w_re, w_im = weight_ref[s, 0], weight_ref[s, 1]
        b_re = dot_t(z[0], w_re) + dot_t(-z[1], w_im)
        b_im = dot_t(z[0], w_im) + dot_t(z[1], w_re)
        both = jnp.concatenate([b_re, b_im], 0).astype(BF)
        beam_buf[b] = dot(frames_ref[...], both).astype(BF).reshape(128, 2, BEAMS)
        started.append(pltpu.make_async_copy(beam_buf.at[b], beam.at[s], beam_sem.at[b]))
        started[-1].start()
        copies[s] = started
    for started in copies.values():
        for copy in started:
            copy.wait()


def make_outputs(flags, got, weights):
    frames = jnp.asarray(frame_order(), BF)
    return pl.pallas_call(
        pair_kernel,
        in_specs=[VM] * 3 + [HB],
        out_specs=[ANY, ANY],
        out_shape=[
            jax.ShapeDtypeStruct((SLOTS, 2, INPUTS, INPUTS), BF),
            jax.ShapeDtypeStruct((SLOTS, 128, 2, BEAMS), BF),
        ],
        scratch_shapes=[
            pltpu.VMEM((16, 512, 128), F32),
            pltpu.VMEM((SLOTS, 2, INPUTS, INPUTS), BF),
            pltpu.VMEM((SLOTS, 128, 2, BEAMS), BF),
            pltpu.VMEM((SLOTS, 2, BEAMS, INPUTS), BF),
            pltpu.SemaphoreType.DMA((SLOTS, 2)),
            pltpu.SemaphoreType.DMA((SLOTS,)),
            pltpu.SemaphoreType.DMA((SLOTS,)),
        ],
        compiler_params=pltpu.CompilerParams(vmem_limit_bytes=24 * MIB),
        cost_estimate=pl.CostEstimate(flops=5_000_000_000, transcendentals=0, bytes_accessed=16 * MIB),
        name="pairs",
    )(flags, frames, got, pltpu.with_memory_space_constraint(weights, pltpu.HBM))


def shards(voltages, station_flags, owner_map, beam_table, table_gains, table_delays):
    n_time = lax.axis_size("tm")
    up = lambda x: lax.ppermute(x, "tm", [(i, (i + 1) % n_time) for i in range(n_time)])
    down = lambda x: lax.ppermute(x, "tm", [(i, (i - 1) % n_time) for i in range(n_time)])
    down0, up0, down1, up1 = cut(voltages, [(0, 4), (13, 16), (4, 8), (9, 13)], "cut")
    n1, p1 = down(down0), up(up0)
    n2, p2 = down(down1), up(up1)
    cos, sin = make_table(owner_map)
    taps = jnp.asarray(taps_table())
    first, held = make_spectra(0, (voltages, p1, n1, taps, cos, sin))
    spectra = make_spectra(1, (p2, n2, taps, cos, sin, held), first)
    weights = make_weights(owner_map, beam_table, table_gains, table_delays)
    flags = jnp.repeat(station_flags, 2).astype(F32).reshape(1, INPUTS)
    got = lax.all_to_all(spectra, ("freq", "tm"), split_axis=0, concat_axis=0, tiled=True)
    return make_outputs(flags, got, weights)


def solution(mesh):
    in_specs = (P("freq", "tm"), P(), P(), P(), P(), P())
    out_specs = (P(("tm", "freq"), None, None, None), P(("tm", "freq"), None, None, None))
    return jax.shard_map(shards, mesh=mesh, in_specs=in_specs, out_specs=out_specs, check_vma=False)
```

```python
import functools
import math

import jax
import jax.numpy as jnp
import numpy as np
from jax import lax
from jax.experimental import pallas as pl
from jax.experimental.pallas import tpu as pltpu
from jax.sharding import PartitionSpec as P

INPUTS = 512
CH = 1024
L = 2048
TAPS = 16
BEAMS = 256
NTAB = 256
FR = 16
IN_DEV = 32
SLOTS = 8
BF = jnp.bfloat16
F32 = jnp.float32
MIB = 1 << 20
VM = pl.BlockSpec(memory_space=pltpu.VMEM)
SM = pl.BlockSpec(memory_space=pltpu.SMEM)
ANY = pl.BlockSpec(memory_space=pl.ANY)
HB = pl.BlockSpec(memory_space=pltpu.HBM)


def fit(fn, degree):
    nodes = np.cos(np.pi * (np.arange(64) + 0.5) / 64) * 0.125 + 0.125
    poly = np.polynomial.Chebyshev.fit(nodes, fn(np.sqrt(nodes)), degree, domain=[0.0, 0.25])
    return [float(c) for c in poly.convert(kind=np.polynomial.Polynomial).coef]


COS = fit(lambda r: np.cos(2 * np.pi * r), 6)
NEG_SIN = fit(lambda r: -np.sin(2 * np.pi * r) / r, 5)


def horner(coefs, z):
    total = z * coefs[-1] + coefs[-2]
    for c in coefs[-3::-1]:
        total = total * z + c
    return total


def cos_negsin(turns):
    r = turns - jnp.floor(turns + 0.5)
    z = r * r
    return horner(COS, z), horner(NEG_SIN, z) * r


def taps_table():
    index = np.arange(TAPS * L).astype(np.float64)
    offset = (index - TAPS * L / 2 + 0.5) / L
    window = 0.5 - 0.5 * np.cos(2.0 * np.pi * (index + 0.5) / (TAPS * L))
    return (np.sinc(offset) * window).reshape(TAPS, L).astype(np.float32)


def lane_order():
    row = lax.broadcasted_iota(jnp.int32, (512, 512), 0)
    column = lax.broadcasted_iota(jnp.int32, (512, 512), 1)
    goal = ((row >> 5) & 3) * 128 + (row >> 7) * 32 + (row & 31)
    return (goal == column).astype(F32).astype(BF)


def frames_of(phase):
    return [4 + u for u in range(8)] if phase == 0 else [0, 1, 2, 3, 12, 13, 14, 15]


def frame_order():
    m = np.zeros((256, 256), np.float32)
    for c in range(2):
        for tl in range(4):
            for tm in range(8):
                for ph in range(2):
                    for th in range(2):
                        o = frames_of(ph)[th * 4 + tl]
                        t = (tm * FR + 8 + o) % 128
                        m[t * 2 + c, c * 128 + tl * 32 + tm * 4 + ph * 2 + th] = 1
    return m


def table_kernel(owner_ref, cos_ref, sin_ref, chans):
    turned = owner_ref[...].astype(F32).T
    for f in range(16):
        for t in range(8):
            column = turned[f * SLOTS : (f + 1) * SLOTS, t : t + 1]
            chans[f * 64 + t * SLOTS : f * 64 + (t + 1) * SLOTS, :] = jnp.broadcast_to(column, (SLOTS, 128))

    def group(g, carry):
        chan = chans[pl.ds(pl.multiple_of(g * 64, 64), 64), :]
        n2 = lax.broadcasted_iota(jnp.int32, (64, 128), 1).astype(F32)
        c, s = cos_negsin(chan * n2 * (1.0 / L))
        a, b = cos_negsin(chan * (128.0 / L))
        at = pl.ds(pl.multiple_of(g * 64, 64), 64)
        for n1 in range(L // 128):
            cos_ref[at, n1 * 128 : (n1 + 1) * 128] = c.astype(BF)
            sin_ref[at, n1 * 128 : (n1 + 1) * 128] = s.astype(BF)
            if n1 < L // 128 - 1:
                c, s = c * a - s * b, s * a + c * b
        return carry

    lax.fori_loop(0, 16, group, 0)


def make_table(owner_map):
    return pl.pallas_call(
        table_kernel,
        in_specs=[VM],
        out_specs=[VM, VM],
        out_shape=[pltpu.VMEM((CH, L), BF)] * 2,
        scratch_shapes=[pltpu.VMEM((CH, 128), F32)],
        cost_estimate=pl.CostEstimate(flops=16 * CH * L, transcendentals=0, bytes_accessed=8 * MIB),
        compiler_params=pltpu.CompilerParams(vmem_limit_bytes=4 * MIB),
        name="table",
    )(owner_map.reshape(8, 128))


def weight_kernel(owner_ref, beam_ref, gains_ref, delays_ref, out_ref, gain, delay):
    def pick(g, carry):
        for j in range(8):
            b = g * 8 + j
            row = beam_ref[b]
            gain[pl.ds(b, 1), :] = gains_ref[pl.ds(row, 1), :]
            delay[pl.ds(b, 1), :] = delays_ref[pl.ds(row, 1), :]
        return carry

    lax.fori_loop(0, BEAMS // 8, pick, 0)
    start = (lax.axis_index("tm") * 16 + lax.axis_index("freq")) * SLOTS

    def group(g, carry):
        s = g // (BEAMS // 64)
        at = pl.ds(pl.multiple_of(g % (BEAMS // 64) * 64, 64), 64)
        chan = owner_ref[start + s].astype(F32) * (1.0 / L)
        c, n = cos_negsin(delay[at, :] * chan)
        scaled = gain[at, :] * (1.0 / math.sqrt(INPUTS))
        out_ref[s, 0, at, :] = (scaled * c).astype(BF)
        out_ref[s, 1, at, :] = (scaled * n).astype(BF)
        return carry

    lax.fori_loop(0, SLOTS * BEAMS // 64, group, 0)


def make_weights(owner_map, beam_table, gains, delays):
    return pl.pallas_call(
        weight_kernel,
        in_specs=[SM, SM, VM, VM],
        out_specs=VM,
        out_shape=pltpu.VMEM((SLOTS, 2, BEAMS, INPUTS), BF),
        scratch_shapes=[pltpu.VMEM((BEAMS, INPUTS), F32)] * 2,
        cost_estimate=pl.CostEstimate(flops=50 * SLOTS * INPUTS * BEAMS, transcendentals=0, bytes_accessed=6 * MIB),
        compiler_params=pltpu.CompilerParams(vmem_limit_bytes=4 * MIB),
        name="weights",
    )(owner_map, beam_table, gains, delays)


def cut_kernel(firsts, source, *refs):
    outs, sem = refs[:-1], refs[-1]
    copies = [
        pltpu.make_async_copy(source.at[:, pl.ds(first * L, out.shape[1])], out, sem.at[i])
        for i, (first, out) in enumerate(zip(firsts, outs))
    ]
    for copy in copies:
        copy.start()
    for copy in copies:
        copy.wait()


def cut(voltages, ranges, name):
    return pl.pallas_call(
        functools.partial(cut_kernel, [a for a, _ in ranges]),
        in_specs=[HB],
        out_specs=[VM] * len(ranges),
        out_shape=[pltpu.VMEM((IN_DEV, (b - a) * L), BF) for a, b in ranges],
        scratch_shapes=[pltpu.SemaphoreType.DMA((len(ranges),))],
        compiler_params=pltpu.CompilerParams(vmem_limit_bytes=4 * MIB),
        cost_estimate=pl.CostEstimate(flops=0, transcendentals=0, bytes_accessed=2 * MIB),
        name=name,
    )(pltpu.with_memory_space_constraint(voltages, pltpu.HBM))


def spectra_kernel(phase, *refs):
    if phase == 0:
        own, p1, n1, taps_ref, cos_ref, sin_ref, *_, out, held, filt, message, sem = refs
        p2 = n2 = None
    else:
        p2, n2, taps_ref, cos_ref, sin_ref, held, *_, out, filt, message, sem = refs
        own = p1 = n1 = None
    pieces = [(p2, f) for f in range(4)] + [(p1, f) for f in range(3)] + [(own, f) for f in range(FR)]
    pieces += [(n1, f) for f in range(4)] + [(n2, f) for f in range(4)]
    now = frames_of(phase)
    later = frames_of(1)
    wanted = now + later if phase == 0 else now
    tm = lax.axis_index("tm")
    after_first = (tm != 0).astype(F32)
    before_last = (tm != lax.axis_size("tm") - 1).astype(F32)

    def column(j, carry):
        at = pl.multiple_of(j * 128, 128)
        lanes = pl.ds(at, 128)
        taps = [taps_ref[k : k + 1, lanes] for k in range(TAPS)]
        for g in range(IN_DEV // 16):
            rows = lambda o, among: slice(among.index(o) * IN_DEV + g * 16, among.index(o) * IN_DEV + g * 16 + 16)
            acc = {}
            for f, (ref, i) in enumerate(pieces):
                if f == 7:
                    for o in acc:
                        acc[o] = acc[o] * after_first
                    if phase == 1:
                        for o in now:
                            held_o = held[rows(o, later), lanes]
                            acc[o] = acc[o] + held_o if o in acc else held_o
                if f == 23 and phase == 0:
                    for o in acc:
                        if o >= 8:
                            acc[o] = acc[o] * before_last
                hit = [o for o in wanted if o <= f < o + TAPS]
                if ref is not None and hit:
                    x = ref[g * 16 : g * 16 + 16, pl.ds(i * L + at, 128)].astype(F32)
                    for o in hit:
                        term = taps[f - o] * x
                        acc[o] = acc[o] + term if o in acc else term
                for o in hit:
                    if o == f - TAPS + 1 and o in now:
                        filt[rows(o, now), lanes] = acc.pop(o).astype(BF)
                    elif o in later and phase == 0 and f == min(o + TAPS - 1, 26):
                        held[rows(o, later), lanes] = acc.pop(o)
        return carry

    lax.fori_loop(0, L // 128, column, 0)
    copies = []
    for q in range(4):
        rows = slice(q * 256, q * 256 + 256)
        dot = lambda ref: lax.dot_general(
            ref[rows, :], filt[...], (((1,), (1,)), ((), ())), preferred_element_type=F32
        ) * (1.0 / math.sqrt(L))
        re, im = dot(cos_ref), dot(sin_ref)
        for th in range(2):
            lanes = slice(th * 128, th * 128 + 128)
            both = [re[:, lanes].reshape(32, SLOTS, 128), im[:, lanes].reshape(32, SLOTS, 128)]
            message[q * 32 : q * 32 + 32, th * 16 : th * 16 + 16, :] = jnp.concatenate(both, 1).astype(BF)
        at = pl.ds(q * 32, 32)
        copies.append(pltpu.make_async_copy(message.at[at], out.at[at, pl.ds(phase * 32, 32)], sem.at[q]))
        copies[-1].start()
    for copy in copies:
        copy.wait()


def make_spectra(phase, args, after=()):
    ready = len(args)
    args = [*args, *after]
    out = pltpu.VMEM((128, 64, 128), BF)
    return pl.pallas_call(
        functools.partial(spectra_kernel, phase),
        in_specs=[VM] * ready + [ANY] * len(after),
        out_specs=ANY if phase else [ANY, VM],
        out_shape=out if phase else [out, pltpu.VMEM((8 * IN_DEV, L), F32)],
        input_output_aliases={len(args) - 1: 0} if phase else {},
        scratch_shapes=[
            pltpu.VMEM((8 * IN_DEV, L), BF),
            pltpu.VMEM((128, 32, 128), BF),
            pltpu.SemaphoreType.DMA((4,)),
        ],
        compiler_params=pltpu.CompilerParams(vmem_limit_bytes=8 * MIB),
        cost_estimate=pl.CostEstimate(flops=4 * CH * L * 256, transcendentals=0, bytes_accessed=12 * MIB),
        name="spectra%d" % phase,
    )(*args)


def pair_kernel(
    flag_ref, frames_ref, got_ref, weight_ref, vis, beam, y, vis_buf, beam_buf, sem, beam_sem
):
    dot = functools.partial(jnp.dot, preferred_element_type=F32)
    dot_t = lambda a, b: lax.dot_general(a, b, (((1,), (1,)), ((), ())), preferred_element_type=F32)
    lanes = lane_order()
    station = lax.broadcasted_iota(jnp.int32, (INPUTS // 2, INPUTS), 0)
    twice = (station == lax.broadcasted_iota(jnp.int32, (INPUTS // 2, INPUTS), 1) >> 1).astype(F32).astype(BF)
    used = jnp.broadcast_to(flag_ref[...].astype(F32), (8, INPUTS // 2)).astype(BF)
    flags = dot(used, twice)[0:1]
    for fh in range(4):
        parts = [got_ref[(fh * 4 + fl) * 8 : (fh * 4 + fl) * 8 + 8].reshape(512, 128) for fl in range(4)]
        block = dot(jnp.concatenate(parts, 1), lanes)
        flag = flags[:, fh * 128 : (fh + 1) * 128]
        for tl in range(4):
            y[fh * 4 + tl] = block[:, tl * 128 : (tl + 1) * 128] * flag
    copies = {}
    for s in range(SLOTS):
        b = s
        z = [
            jnp.concatenate(
                [
                    jnp.concatenate([y[fh * 4 + tl, pl.ds(r * 8 + s, 32, stride=16), :] for fh in range(4)], 1)
                    for tl in range(4)
                ],
                0,
            ).astype(BF)
            for r in range(2)
        ]
        w = jnp.concatenate(z, 0)
        wt = w.T
        vt = jnp.concatenate([wt[:, 128:], -wt[:, :128]], 1)
        started = []
        for c, left in enumerate((wt, vt)):
            vis_buf[b, c] = (dot(left, w) * (1.0 / 128)).astype(BF)
            started.append(pltpu.make_async_copy(vis_buf.at[b, c], vis.at[s, c], sem.at[b, c]))
            started[-1].start()
        w_re, w_im = weight_ref[s, 0], weight_ref[s, 1]
        by_re, by_im = dot_t(w, w_re), dot_t(w, w_im)
        b_re = by_re[:128] - by_im[128:]
        b_im = by_im[:128] + by_re[128:]
        both = jnp.concatenate([b_re, b_im], 0).astype(BF)
        beam_buf[b] = dot(frames_ref[...], both).astype(BF).reshape(128, 2, BEAMS)
        started.append(pltpu.make_async_copy(beam_buf.at[b], beam.at[s], beam_sem.at[b]))
        started[-1].start()
        copies[s] = started
    for started in copies.values():
        for copy in started:
            copy.wait()


def make_outputs(flags, got, weights):
    frames = jnp.asarray(frame_order(), BF)
    return pl.pallas_call(
        pair_kernel,
        in_specs=[VM] * 4,
        out_specs=[ANY, ANY],
        out_shape=[
            jax.ShapeDtypeStruct((SLOTS, 2, INPUTS, INPUTS), BF),
            jax.ShapeDtypeStruct((SLOTS, 128, 2, BEAMS), BF),
        ],
        scratch_shapes=[
            pltpu.VMEM((16, 512, 128), F32),
            pltpu.VMEM((SLOTS, 2, INPUTS, INPUTS), BF),
            pltpu.VMEM((SLOTS, 128, 2, BEAMS), BF),
            pltpu.SemaphoreType.DMA((SLOTS, 2)),
            pltpu.SemaphoreType.DMA((SLOTS,)),
        ],
        compiler_params=pltpu.CompilerParams(vmem_limit_bytes=20 * MIB),
        cost_estimate=pl.CostEstimate(flops=5_000_000_000, transcendentals=0, bytes_accessed=16 * MIB),
        name="pairs",
    )(flags, frames, got, weights)


def shards(voltages, station_flags, owner_map, beam_table, table_gains, table_delays):
    n_time = lax.axis_size("tm")
    up = lambda x: lax.ppermute(x, "tm", [(i, (i + 1) % n_time) for i in range(n_time)])
    down = lambda x: lax.ppermute(x, "tm", [(i, (i - 1) % n_time) for i in range(n_time)])
    down0, up0, down1, up1 = cut(voltages, [(0, 4), (13, 16), (4, 8), (9, 13)], "cut")
    n1, p1 = down(down0), up(up0)
    n2, p2 = down(down1), up(up1)
    cos, sin = make_table(owner_map)
    taps = jnp.asarray(taps_table())
    weights = make_weights(owner_map, beam_table, table_gains, table_delays)
    flags = station_flags.reshape(1, INPUTS // 2)
    first, held = make_spectra(0, (voltages, p1, n1, taps, cos, sin), (weights,))
    spectra = make_spectra(1, (p2, n2, taps, cos, sin, held), (first,))
    got = lax.all_to_all(spectra, ("freq", "tm"), split_axis=0, concat_axis=0, tiled=True)
    return make_outputs(flags, got, weights)


def solution(mesh):
    in_specs = (P("freq", "tm"), P(), P(), P(), P(), P())
    out_specs = (P(("tm", "freq"), None, None, None), P(("tm", "freq"), None, None, None))
    return jax.shard_map(shards, mesh=mesh, in_specs=in_specs, out_specs=out_specs, check_vma=False)
```

```python
import functools
import math

import jax
import jax.numpy as jnp
import numpy as np
from jax import lax
from jax.experimental import pallas as pl
from jax.experimental.pallas import tpu as pltpu
from jax.sharding import PartitionSpec as P

INPUTS = 512
CH = 1024
L = 2048
TAPS = 16
BEAMS = 256
NTAB = 256
FR = 16
IN_DEV = 32
SLOTS = 8
BF = jnp.bfloat16
F32 = jnp.float32
MIB = 1 << 20
VM = pl.BlockSpec(memory_space=pltpu.VMEM)
SM = pl.BlockSpec(memory_space=pltpu.SMEM)
ANY = pl.BlockSpec(memory_space=pl.ANY)
HB = pl.BlockSpec(memory_space=pltpu.HBM)


def fit(fn, degree):
    nodes = np.cos(np.pi * (np.arange(64) + 0.5) / 64) * 0.125 + 0.125
    poly = np.polynomial.Chebyshev.fit(nodes, fn(np.sqrt(nodes)), degree, domain=[0.0, 0.25])
    return [float(c) for c in poly.convert(kind=np.polynomial.Polynomial).coef]


COS = fit(lambda r: np.cos(2 * np.pi * r), 6)
NEG_SIN = fit(lambda r: -np.sin(2 * np.pi * r) / r, 5)


def horner(coefs, z):
    total = z * coefs[-1] + coefs[-2]
    for c in coefs[-3::-1]:
        total = total * z + c
    return total


def cos_negsin(turns):
    r = turns - jnp.floor(turns + 0.5)
    z = r * r
    return horner(COS, z), horner(NEG_SIN, z) * r


def taps_table():
    index = np.arange(TAPS * L).astype(np.float64)
    offset = (index - TAPS * L / 2 + 0.5) / L
    window = 0.5 - 0.5 * np.cos(2.0 * np.pi * (index + 0.5) / (TAPS * L))
    return (np.sinc(offset) * window).reshape(TAPS, L).astype(np.float32)


def lane_order():
    m = np.zeros((512, 512), np.float32)
    for fl in range(4):
        for tl in range(4):
            for i in range(32):
                m[fl * 128 + tl * 32 + i, tl * 128 + fl * 32 + i] = 1
    return m


def frames_of(phase):
    return [4 + u for u in range(8)] if phase == 0 else [0, 1, 2, 3, 12, 13, 14, 15]


def frame_order():
    m = np.zeros((256, 256), np.float32)
    for c in range(2):
        for tl in range(4):
            for tm in range(8):
                for ph in range(2):
                    for th in range(2):
                        o = frames_of(ph)[th * 4 + tl]
                        t = (tm * FR + 8 + o) % 128
                        m[t * 2 + c, c * 128 + tl * 32 + tm * 4 + ph * 2 + th] = 1
    return m


def table_kernel(owner_ref, cos_ref, sin_ref, chans):
    turned = owner_ref[...].astype(F32).T
    for f in range(16):
        for t in range(8):
            column = turned[f * SLOTS : (f + 1) * SLOTS, t : t + 1]
            chans[f * 64 + t * SLOTS : f * 64 + (t + 1) * SLOTS, :] = jnp.broadcast_to(column, (SLOTS, 128))

    def group(g, carry):
        chan = chans[pl.ds(pl.multiple_of(g * 64, 64), 64), :]
        n2 = lax.broadcasted_iota(jnp.int32, (64, 128), 1).astype(F32)
        c, s = cos_negsin(chan * n2 * (1.0 / L))
        a, b = cos_negsin(chan * (128.0 / L))
        at = pl.ds(pl.multiple_of(g * 64, 64), 64)
        for n1 in range(L // 128):
            cos_ref[at, n1 * 128 : (n1 + 1) * 128] = c.astype(BF)
            sin_ref[at, n1 * 128 : (n1 + 1) * 128] = s.astype(BF)
            if n1 < L // 128 - 1:
                c, s = c * a - s * b, s * a + c * b
        return carry

    lax.fori_loop(0, 16, group, 0)


def make_table(owner_map):
    return pl.pallas_call(
        table_kernel,
        in_specs=[VM],
        out_specs=[VM, VM],
        out_shape=[pltpu.VMEM((CH, L), BF)] * 2,
        scratch_shapes=[pltpu.VMEM((CH, 128), F32)],
        cost_estimate=pl.CostEstimate(flops=16 * CH * L, transcendentals=0, bytes_accessed=8 * MIB),
        compiler_params=pltpu.CompilerParams(vmem_limit_bytes=4 * MIB),
        name="table",
    )(owner_map.reshape(8, 128))


def weight_kernel(owner_ref, beam_ref, gains_ref, delays_ref, out_ref, gain, delay):
    def pick(g, carry):
        for j in range(8):
            b = g * 8 + j
            row = beam_ref[b]
            gain[pl.ds(b, 1), :] = gains_ref[pl.ds(row, 1), :]
            delay[pl.ds(b, 1), :] = delays_ref[pl.ds(row, 1), :]
        return carry

    lax.fori_loop(0, BEAMS // 8, pick, 0)
    start = (lax.axis_index("tm") * 16 + lax.axis_index("freq")) * SLOTS

    def group(g, carry):
        s = g // (BEAMS // 64)
        at = pl.ds(pl.multiple_of(g % (BEAMS // 64) * 64, 64), 64)
        chan = owner_ref[start + s].astype(F32) * (1.0 / L)
        c, n = cos_negsin(delay[at, :] * chan)
        scaled = gain[at, :] * (1.0 / math.sqrt(INPUTS))
        out_ref[s, 0, at, :] = (scaled * c).astype(BF)
        out_ref[s, 1, at, :] = (scaled * n).astype(BF)
        return carry

    lax.fori_loop(0, SLOTS * BEAMS // 64, group, 0)


def make_weights(owner_map, beam_table, gains, delays):
    return pl.pallas_call(
        weight_kernel,
        in_specs=[SM, SM, VM, VM],
        out_specs=VM,
        out_shape=pltpu.VMEM((SLOTS, 2, BEAMS, INPUTS), BF),
        scratch_shapes=[pltpu.VMEM((BEAMS, INPUTS), F32)] * 2,
        cost_estimate=pl.CostEstimate(flops=50 * SLOTS * INPUTS * BEAMS, transcendentals=0, bytes_accessed=6 * MIB),
        compiler_params=pltpu.CompilerParams(vmem_limit_bytes=4 * MIB),
        name="weights",
    )(owner_map, beam_table, gains, delays)


def cut_kernel(firsts, source, *refs):
    outs, sem = refs[:-1], refs[-1]
    copies = [
        pltpu.make_async_copy(source.at[:, pl.ds(first * L, out.shape[1])], out, sem.at[i])
        for i, (first, out) in enumerate(zip(firsts, outs))
    ]
    for copy in copies:
        copy.start()
    for copy in copies:
        copy.wait()


def cut(voltages, ranges, name):
    return pl.pallas_call(
        functools.partial(cut_kernel, [a for a, _ in ranges]),
        in_specs=[HB],
        out_specs=[VM] * len(ranges),
        out_shape=[pltpu.VMEM((IN_DEV, (b - a) * L), BF) for a, b in ranges],
        scratch_shapes=[pltpu.SemaphoreType.DMA((len(ranges),))],
        compiler_params=pltpu.CompilerParams(vmem_limit_bytes=4 * MIB),
        cost_estimate=pl.CostEstimate(flops=0, transcendentals=0, bytes_accessed=2 * MIB),
        name=name,
    )(pltpu.with_memory_space_constraint(voltages, pltpu.HBM))


def spectra_kernel(phase, *refs):
    if phase == 0:
        own, p1, n1, taps_ref, cos_ref, sin_ref, *_, out, held, filt, message, sem = refs
        p2 = n2 = None
    else:
        p2, n2, taps_ref, cos_ref, sin_ref, held, *_, out, filt, message, sem = refs
        own = p1 = n1 = None
    pieces = [(p2, f) for f in range(4)] + [(p1, f) for f in range(3)] + [(own, f) for f in range(FR)]
    pieces += [(n1, f) for f in range(4)] + [(n2, f) for f in range(4)]
    now = frames_of(phase)
    later = frames_of(1)
    wanted = now + later if phase == 0 else now
    tm = lax.axis_index("tm")
    after_first = (tm != 0).astype(F32)
    before_last = (tm != lax.axis_size("tm") - 1).astype(F32)

    def column(j, carry):
        at = pl.multiple_of(j * 128, 128)
        lanes = pl.ds(at, 128)
        taps = [taps_ref[k : k + 1, lanes] for k in range(TAPS)]
        for g in range(IN_DEV // 16):
            rows = lambda o, among: slice(among.index(o) * IN_DEV + g * 16, among.index(o) * IN_DEV + g * 16 + 16)
            acc = {}
            for f, (ref, i) in enumerate(pieces):
                if f == 7:
                    for o in acc:
                        acc[o] = acc[o] * after_first
                    if phase == 1:
                        for o in now:
                            held_o = held[rows(o, later), lanes]
                            acc[o] = acc[o] + held_o if o in acc else held_o
                if f == 23 and phase == 0:
                    for o in acc:
                        if o >= 8:
                            acc[o] = acc[o] * before_last
                hit = [o for o in wanted if o <= f < o + TAPS]
                if ref is not None and hit:
                    x = ref[g * 16 : g * 16 + 16, pl.ds(i * L + at, 128)].astype(F32)
                    for o in hit:
                        term = taps[f - o] * x
                        acc[o] = acc[o] + term if o in acc else term
                for o in hit:
                    if o == f - TAPS + 1 and o in now:
                        filt[rows(o, now), lanes] = acc.pop(o).astype(BF)
                    elif o in later and phase == 0 and f == min(o + TAPS - 1, 26):
                        held[rows(o, later), lanes] = acc.pop(o)
        return carry

    lax.fori_loop(0, L // 128, column, 0)
    copies = []
    for q in range(4):
        rows = slice(q * 256, q * 256 + 256)
        dot = lambda ref: lax.dot_general(
            ref[rows, :], filt[...], (((1,), (1,)), ((), ())), preferred_element_type=F32
        ) * (1.0 / math.sqrt(L))
        re, im = dot(cos_ref), dot(sin_ref)
        for th in range(2):
            lanes = slice(th * 128, th * 128 + 128)
            both = [re[:, lanes].reshape(32, SLOTS, 128), im[:, lanes].reshape(32, SLOTS, 128)]
            message[q * 32 : q * 32 + 32, th * 16 : th * 16 + 16, :] = jnp.concatenate(both, 1).astype(BF)
        at = pl.ds(q * 32, 32)
        copies.append(pltpu.make_async_copy(message.at[at], out.at[at, pl.ds(phase * 32, 32)], sem.at[q]))
        copies[-1].start()
    for copy in copies:
        copy.wait()


def make_spectra(phase, args, after=()):
    ready = len(args)
    args = [*args, *after]
    out = pltpu.VMEM((128, 64, 128), BF)
    return pl.pallas_call(
        functools.partial(spectra_kernel, phase),
        in_specs=[VM] * ready + [ANY] * len(after),
        out_specs=ANY if phase else [ANY, VM],
        out_shape=out if phase else [out, pltpu.VMEM((8 * IN_DEV, L), F32)],
        input_output_aliases={len(args) - 1: 0} if phase else {},
        scratch_shapes=[
            pltpu.VMEM((8 * IN_DEV, L), BF),
            pltpu.VMEM((128, 32, 128), BF),
            pltpu.SemaphoreType.DMA((4,)),
        ],
        compiler_params=pltpu.CompilerParams(vmem_limit_bytes=8 * MIB),
        cost_estimate=pl.CostEstimate(flops=4 * CH * L * 256, transcendentals=0, bytes_accessed=12 * MIB),
        name="spectra%d" % phase,
    )(*args)


def pair_kernel(
    flag_ref, twice_ref, lanes_ref, frames_ref, got_ref, weight_ref, vis, beam, y, vis_buf, beam_buf, sem, beam_sem
):
    dot = functools.partial(jnp.dot, preferred_element_type=F32)
    dot_t = lambda a, b: lax.dot_general(a, b, (((1,), (1,)), ((), ())), preferred_element_type=F32)
    used = jnp.broadcast_to(flag_ref[...].astype(F32), (8, INPUTS // 2)).astype(BF)
    flags = dot(used, twice_ref[...])[0:1]
    for fh in range(4):
        parts = [got_ref[(fh * 4 + fl) * 8 : (fh * 4 + fl) * 8 + 8].reshape(512, 128) for fl in range(4)]
        block = dot(jnp.concatenate(parts, 1), lanes_ref[...])
        flag = flags[:, fh * 128 : (fh + 1) * 128]
        for tl in range(4):
            y[fh * 4 + tl] = block[:, tl * 128 : (tl + 1) * 128] * flag
    def prepare(s):
        rows = [pl.ds(r * 8 + s, 32, stride=16) for r in range(2)]
        pieces = [[[y[fh * 4 + tl, at, :] for fh in range(4)] for tl in range(4)] for at in rows]
        w = jnp.concatenate([jnp.concatenate([jnp.concatenate(p, 1) for p in half], 0) for half in pieces], 0).astype(BF)
        return w, w.T

    def finish(s, by):
        b_re = by[:BEAMS, :128] - by[BEAMS:, 128:]
        b_im = by[BEAMS:, :128] + by[:BEAMS, 128:]
        both = jnp.concatenate([b_re, b_im], 1).astype(BF)
        beam_buf[s] = dot_t(frames_ref[...], both).astype(BF).reshape(128, 2, BEAMS)
        copy = pltpu.make_async_copy(beam_buf.at[s], beam.at[s], beam_sem.at[s])
        copy.start()
        return copy

    copies = []
    for s in range(SLOTS):
        w, wt = prepare(s)
        by = dot(weight_ref[s].reshape(2 * BEAMS, INPUTS), wt)
        vt = jnp.concatenate([wt[:, 128:], -wt[:, :128]], 1)
        for c, left in enumerate((wt, vt)):
            vis_buf[s, c] = (dot(left, w) * (1.0 / 128)).astype(BF)
            copies.append(pltpu.make_async_copy(vis_buf.at[s, c], vis.at[s, c], sem.at[s, c]))
            copies[-1].start()
        copies.append(finish(s, by))
    for copy in copies:
        copy.wait()


def make_outputs(flags, got, weights):
    twice = np.repeat(np.eye(INPUTS // 2), 2, 1)
    consts = [jnp.asarray(m, BF) for m in (twice, lane_order(), frame_order())]
    return pl.pallas_call(
        pair_kernel,
        in_specs=[VM] * 6,
        out_specs=[ANY, ANY],
        out_shape=[
            jax.ShapeDtypeStruct((SLOTS, 2, INPUTS, INPUTS), BF),
            jax.ShapeDtypeStruct((SLOTS, 128, 2, BEAMS), BF),
        ],
        scratch_shapes=[
            pltpu.VMEM((16, 512, 128), F32),
            pltpu.VMEM((SLOTS, 2, INPUTS, INPUTS), BF),
            pltpu.VMEM((SLOTS, 128, 2, BEAMS), BF),
            pltpu.SemaphoreType.DMA((SLOTS, 2)),
            pltpu.SemaphoreType.DMA((SLOTS,)),
        ],
        compiler_params=pltpu.CompilerParams(vmem_limit_bytes=20 * MIB),
        cost_estimate=pl.CostEstimate(flops=5_000_000_000, transcendentals=0, bytes_accessed=16 * MIB),
        name="pairs",
    )(flags, *consts, got, weights)


def shards(voltages, station_flags, owner_map, beam_table, table_gains, table_delays):
    n_time = lax.axis_size("tm")
    up = lambda x: lax.ppermute(x, "tm", [(i, (i + 1) % n_time) for i in range(n_time)])
    down = lambda x: lax.ppermute(x, "tm", [(i, (i - 1) % n_time) for i in range(n_time)])
    down0, up0, down1, up1 = cut(voltages, [(0, 4), (13, 16), (4, 8), (9, 13)], "cut")
    n1, p1 = down(down0), up(up0)
    n2, p2 = down(down1), up(up1)
    cos, sin = make_table(owner_map)
    taps = jnp.asarray(taps_table())
    weights = make_weights(owner_map, beam_table, table_gains, table_delays)
    flags = station_flags.reshape(1, INPUTS // 2)
    first, held = make_spectra(0, (voltages, p1, n1, taps, cos, sin), (weights,))
    spectra = make_spectra(1, (p2, n2, taps, cos, sin, held), (first,))
    got = lax.all_to_all(spectra, ("freq", "tm"), split_axis=0, concat_axis=0, tiled=True)
    return make_outputs(flags, got, weights)


def solution(mesh):
    in_specs = (P("freq", "tm"), P(), P(), P(), P(), P())
    out_specs = (P(("tm", "freq"), None, None, None), P(("tm", "freq"), None, None, None))
    return jax.shard_map(shards, mesh=mesh, in_specs=in_specs, out_specs=out_specs, check_vma=False)
```

```python
import functools
import math

import jax
import jax.numpy as jnp
import numpy as np
from jax import lax
from jax.experimental import pallas as pl
from jax.experimental.pallas import tpu as pltpu
from jax.sharding import PartitionSpec as P

INPUTS = 512
CH = 1024
L = 2048
TAPS = 16
BEAMS = 256
NTAB = 256
FR = 16
IN_DEV = 32
SLOTS = 8
BF = jnp.bfloat16
F32 = jnp.float32
MIB = 1 << 20
VM = pl.BlockSpec(memory_space=pltpu.VMEM)
SM = pl.BlockSpec(memory_space=pltpu.SMEM)
ANY = pl.BlockSpec(memory_space=pl.ANY)
HB = pl.BlockSpec(memory_space=pltpu.HBM)


def fit(fn, degree):
    nodes = np.cos(np.pi * (np.arange(64) + 0.5) / 64) * 0.125 + 0.125
    poly = np.polynomial.Chebyshev.fit(nodes, fn(np.sqrt(nodes)), degree, domain=[0.0, 0.25])
    return [float(c) for c in poly.convert(kind=np.polynomial.Polynomial).coef]


COS = fit(lambda r: np.cos(2 * np.pi * r), 6)
NEG_SIN = fit(lambda r: -np.sin(2 * np.pi * r) / r, 5)


def horner(coefs, z):
    total = z * coefs[-1] + coefs[-2]
    for c in coefs[-3::-1]:
        total = total * z + c
    return total


def cos_negsin(turns):
    r = turns - jnp.floor(turns + 0.5)
    z = r * r
    return horner(COS, z), horner(NEG_SIN, z) * r


def taps_table():
    index = np.arange(TAPS * L).astype(np.float64)
    offset = (index - TAPS * L / 2 + 0.5) / L
    window = 0.5 - 0.5 * np.cos(2.0 * np.pi * (index + 0.5) / (TAPS * L))
    return (np.sinc(offset) * window).reshape(TAPS, L).astype(np.float32)


def lane_order():
    m = np.zeros((512, 512), np.float32)
    for fl in range(4):
        for tl in range(4):
            for i in range(32):
                m[fl * 128 + tl * 32 + i, tl * 128 + fl * 32 + i] = 1
    return m


def frames_of(phase):
    return [4 + u for u in range(8)] if phase == 0 else [0, 1, 2, 3, 12, 13, 14, 15]


def frame_order():
    m = np.zeros((256, 256), np.float32)
    for c in range(2):
        for tl in range(4):
            for tm in range(8):
                for ph in range(2):
                    for th in range(2):
                        o = frames_of(ph)[th * 4 + tl]
                        t = (tm * FR + 8 + o) % 128
                        m[t * 2 + c, c * 128 + tl * 32 + tm * 4 + ph * 2 + th] = 1
    return m


def table_kernel(owner_ref, cos_ref, sin_ref, chans):
    turned = owner_ref[...].astype(F32).T
    for f in range(16):
        for t in range(8):
            column = turned[f * SLOTS : (f + 1) * SLOTS, t : t + 1]
            chans[f * 64 + t * SLOTS : f * 64 + (t + 1) * SLOTS, :] = jnp.broadcast_to(column, (SLOTS, 128))

    def group(g, carry):
        chan = chans[pl.ds(pl.multiple_of(g * 64, 64), 64), :]
        n2 = lax.broadcasted_iota(jnp.int32, (64, 128), 1).astype(F32)
        c, s = cos_negsin(chan * n2 * (1.0 / L))
        a, b = cos_negsin(chan * (128.0 / L))
        at = pl.ds(pl.multiple_of(g * 64, 64), 64)
        for n1 in range(L // 128):
            cos_ref[at, n1 * 128 : (n1 + 1) * 128] = c.astype(BF)
            sin_ref[at, n1 * 128 : (n1 + 1) * 128] = s.astype(BF)
            if n1 < L // 128 - 1:
                c, s = c * a - s * b, s * a + c * b
        return carry

    lax.fori_loop(0, 16, group, 0)


def make_table(owner_map):
    return pl.pallas_call(
        table_kernel,
        in_specs=[VM],
        out_specs=[VM, VM],
        out_shape=[pltpu.VMEM((CH, L), BF)] * 2,
        scratch_shapes=[pltpu.VMEM((CH, 128), F32)],
        cost_estimate=pl.CostEstimate(flops=16 * CH * L, transcendentals=0, bytes_accessed=8 * MIB),
        compiler_params=pltpu.CompilerParams(vmem_limit_bytes=4 * MIB),
        name="table",
    )(owner_map.reshape(8, 128))


def weight_kernel(owner_ref, beam_ref, gains_ref, delays_ref, out_ref, gain, delay):
    def pick(g, carry):
        for j in range(8):
            b = g * 8 + j
            row = beam_ref[b]
            gain[pl.ds(b, 1), :] = gains_ref[pl.ds(row, 1), :]
            delay[pl.ds(b, 1), :] = delays_ref[pl.ds(row, 1), :]
        return carry

    lax.fori_loop(0, BEAMS // 8, pick, 0)
    start = (lax.axis_index("tm") * 16 + lax.axis_index("freq")) * SLOTS

    def group(g, carry):
        s = g // (BEAMS // 64)
        at = pl.ds(pl.multiple_of(g % (BEAMS // 64) * 64, 64), 64)
        chan = owner_ref[start + s].astype(F32) * (1.0 / L)
        c, n = cos_negsin(delay[at, :] * chan)
        scaled = gain[at, :] * (1.0 / math.sqrt(INPUTS))
        out_ref[s, 0, at, :] = (scaled * c).astype(BF)
        out_ref[s, 1, at, :] = (scaled * n).astype(BF)
        return carry

    lax.fori_loop(0, SLOTS * BEAMS // 64, group, 0)


def make_weights(owner_map, beam_table, gains, delays):
    return pl.pallas_call(
        weight_kernel,
        in_specs=[SM, SM, VM, VM],
        out_specs=VM,
        out_shape=pltpu.VMEM((SLOTS, 2, BEAMS, INPUTS), BF),
        scratch_shapes=[pltpu.VMEM((BEAMS, INPUTS), F32)] * 2,
        cost_estimate=pl.CostEstimate(flops=50 * SLOTS * INPUTS * BEAMS, transcendentals=0, bytes_accessed=6 * MIB),
        compiler_params=pltpu.CompilerParams(vmem_limit_bytes=4 * MIB),
        name="weights",
    )(owner_map, beam_table, gains, delays)


def cut_kernel(firsts, source, *refs):
    outs, sem = refs[:-1], refs[-1]
    copies = [
        pltpu.make_async_copy(source.at[:, pl.ds(first * L, out.shape[1])], out, sem.at[i])
        for i, (first, out) in enumerate(zip(firsts, outs))
    ]
    for copy in copies:
        copy.start()
    for copy in copies:
        copy.wait()


def cut(voltages, ranges, name):
    return pl.pallas_call(
        functools.partial(cut_kernel, [a for a, _ in ranges]),
        in_specs=[HB],
        out_specs=[VM] * len(ranges),
        out_shape=[pltpu.VMEM((IN_DEV, (b - a) * L), BF) for a, b in ranges],
        scratch_shapes=[pltpu.SemaphoreType.DMA((len(ranges),))],
        compiler_params=pltpu.CompilerParams(vmem_limit_bytes=4 * MIB),
        cost_estimate=pl.CostEstimate(flops=0, transcendentals=0, bytes_accessed=2 * MIB),
        name=name,
    )(pltpu.with_memory_space_constraint(voltages, pltpu.HBM))


def spectra_kernel(phase, *refs):
    if phase == 0:
        own, p1, n1, taps_ref, cos_ref, sin_ref, *_, out, held, filt = refs
        p2 = n2 = None
    else:
        p2, n2, taps_ref, cos_ref, sin_ref, held, *_, out, filt = refs
        own = p1 = n1 = None
    pieces = [(p2, f) for f in range(4)] + [(p1, f) for f in range(3)] + [(own, f) for f in range(FR)]
    pieces += [(n1, f) for f in range(4)] + [(n2, f) for f in range(4)]
    now = frames_of(phase)
    later = frames_of(1)
    wanted = now + later if phase == 0 else now
    tm = lax.axis_index("tm")
    after_first = (tm != 0).astype(F32)
    before_last = (tm != lax.axis_size("tm") - 1).astype(F32)

    def column(j, carry):
        at = pl.multiple_of(j * 128, 128)
        lanes = pl.ds(at, 128)
        taps = [taps_ref[k : k + 1, lanes] for k in range(TAPS)]
        for g in range(IN_DEV // 16):
            rows = lambda o, among: slice(among.index(o) * IN_DEV + g * 16, among.index(o) * IN_DEV + g * 16 + 16)
            acc = {}
            for f, (ref, i) in enumerate(pieces):
                if f == 7:
                    for o in acc:
                        acc[o] = acc[o] * after_first
                    if phase == 1:
                        for o in now:
                            held_o = held[rows(o, later), lanes]
                            acc[o] = acc[o] + held_o if o in acc else held_o
                if f == 23 and phase == 0:
                    for o in acc:
                        if o >= 8:
                            acc[o] = acc[o] * before_last
                hit = [o for o in wanted if o <= f < o + TAPS]
                if ref is not None and hit:
                    x = ref[g * 16 : g * 16 + 16, pl.ds(i * L + at, 128)].astype(F32)
                    for o in hit:
                        term = taps[f - o] * x
                        acc[o] = acc[o] + term if o in acc else term
                for o in hit:
                    if o == f - TAPS + 1 and o in now:
                        filt[rows(o, now), lanes] = acc.pop(o).astype(BF)
                    elif o in later and phase == 0 and f == min(o + TAPS - 1, 26):
                        held[rows(o, later), lanes] = acc.pop(o)
        return carry

    lax.fori_loop(0, L // 128, column, 0)
    for q in range(2):
        rows = slice(q * 512, q * 512 + 512)
        dot = lambda ref: lax.dot_general(
            ref[rows, :], filt[...], (((1,), (1,)), ((), ())), preferred_element_type=F32
        ) * (1.0 / math.sqrt(L))
        re, im = dot(cos_ref), dot(sin_ref)
        for th in range(2):
            lanes = slice(th * 128, th * 128 + 128)
            both = [re[:, lanes].reshape(64, SLOTS, 128), im[:, lanes].reshape(64, SLOTS, 128)]
            at = phase * 32 + th * 16
            out[q * 64 : q * 64 + 64, at : at + 16, :] = jnp.concatenate(both, 1).astype(BF)


def make_spectra(phase, args, after=()):
    ready = len(args)
    args = [*args, *after]
    out = pltpu.VMEM((128, 64, 128), BF)
    return pl.pallas_call(
        functools.partial(spectra_kernel, phase),
        in_specs=[VM] * ready + [VM if phase else ANY] * len(after),
        out_specs=VM if phase else [VM, VM],
        out_shape=out if phase else [out, pltpu.VMEM((8 * IN_DEV, L), F32)],
        input_output_aliases={len(args) - 1: 0} if phase else {},
        scratch_shapes=[pltpu.VMEM((8 * IN_DEV, L), BF)],
        compiler_params=pltpu.CompilerParams(vmem_limit_bytes=8 * MIB),
        cost_estimate=pl.CostEstimate(flops=4 * CH * L * 256, transcendentals=0, bytes_accessed=12 * MIB),
        name="spectra%d" % phase,
    )(*args)


def pair_kernel(
    flag_ref, twice_ref, lanes_ref, frames_ref, got_ref, weight_ref, vis, beam, y, vis_buf, beam_buf, sem, beam_sem
):
    dot = functools.partial(jnp.dot, preferred_element_type=F32)
    dot_t = lambda a, b: lax.dot_general(a, b, (((1,), (1,)), ((), ())), preferred_element_type=F32)
    used = jnp.broadcast_to(flag_ref[...].astype(F32), (8, INPUTS // 2)).astype(BF)
    flags = dot(used, twice_ref[...])[0:1]
    for fh in range(4):
        parts = [got_ref[(fh * 4 + fl) * 8 : (fh * 4 + fl) * 8 + 8].reshape(512, 128) for fl in range(4)]
        block = dot(jnp.concatenate(parts, 1), lanes_ref[...])
        flag = flags[:, fh * 128 : (fh + 1) * 128]
        for tl in range(4):
            y[fh * 4 + tl] = block[:, tl * 128 : (tl + 1) * 128] * flag
    def prepare(s):
        rows = [pl.ds(r * 8 + s, 32, stride=16) for r in range(2)]
        pieces = [[[y[fh * 4 + tl, at, :] for fh in range(4)] for tl in range(4)] for at in rows]
        w = jnp.concatenate([jnp.concatenate([jnp.concatenate(p, 1) for p in half], 0) for half in pieces], 0).astype(BF)
        return w, w.T

    def finish(s, by):
        b_re = by[:BEAMS, :128] - by[BEAMS:, 128:]
        b_im = by[BEAMS:, :128] + by[:BEAMS, 128:]
        both = jnp.concatenate([b_re, b_im], 1).astype(BF)
        beam_buf[s] = dot_t(frames_ref[...], both).astype(BF).reshape(128, 2, BEAMS)
        copy = pltpu.make_async_copy(beam_buf.at[s], beam.at[s], beam_sem.at[s])
        copy.start()
        return copy

    copies = []
    for s in range(SLOTS):
        w, wt = prepare(s)
        by = dot(weight_ref[s].reshape(2 * BEAMS, INPUTS), wt)
        vt = jnp.concatenate([wt[:, 128:], -wt[:, :128]], 1)
        for c, left in enumerate((wt, vt)):
            vis_buf[s, c] = (dot(left, w) * (1.0 / 128)).astype(BF)
            copies.append(pltpu.make_async_copy(vis_buf.at[s, c], vis.at[s, c], sem.at[s, c]))
            copies[-1].start()
        copies.append(finish(s, by))
    for copy in copies:
        copy.wait()


def make_outputs(flags, got, weights):
    twice = np.repeat(np.eye(INPUTS // 2), 2, 1)
    consts = [jnp.asarray(m, BF) for m in (twice, lane_order(), frame_order())]
    return pl.pallas_call(
        pair_kernel,
        in_specs=[VM] * 6,
        out_specs=[ANY, ANY],
        out_shape=[
            jax.ShapeDtypeStruct((SLOTS, 2, INPUTS, INPUTS), BF),
            jax.ShapeDtypeStruct((SLOTS, 128, 2, BEAMS), BF),
        ],
        scratch_shapes=[
            pltpu.VMEM((16, 512, 128), F32),
            pltpu.VMEM((SLOTS, 2, INPUTS, INPUTS), BF),
            pltpu.VMEM((SLOTS, 128, 2, BEAMS), BF),
            pltpu.SemaphoreType.DMA((SLOTS, 2)),
            pltpu.SemaphoreType.DMA((SLOTS,)),
        ],
        compiler_params=pltpu.CompilerParams(vmem_limit_bytes=20 * MIB),
        cost_estimate=pl.CostEstimate(flops=5_000_000_000, transcendentals=0, bytes_accessed=16 * MIB),
        name="pairs",
    )(flags, *consts, got, weights)


def shards(voltages, station_flags, owner_map, beam_table, table_gains, table_delays):
    n_time = lax.axis_size("tm")
    up = lambda x: lax.ppermute(x, "tm", [(i, (i + 1) % n_time) for i in range(n_time)])
    down = lambda x: lax.ppermute(x, "tm", [(i, (i - 1) % n_time) for i in range(n_time)])
    down0, up0, down1, up1 = cut(voltages, [(0, 4), (13, 16), (4, 8), (9, 13)], "cut")
    n1, p1 = down(down0), up(up0)
    n2, p2 = down(down1), up(up1)
    cos, sin = make_table(owner_map)
    taps = jnp.asarray(taps_table())
    weights = make_weights(owner_map, beam_table, table_gains, table_delays)
    flags = station_flags.reshape(1, INPUTS // 2)
    first, held = make_spectra(0, (voltages, p1, n1, taps, cos, sin), (weights,))
    spectra = make_spectra(1, (p2, n2, taps, cos, sin, held), (first,))
    got = lax.all_to_all(spectra, ("freq", "tm"), split_axis=0, concat_axis=0, tiled=True)
    return make_outputs(flags, got, weights)


def solution(mesh):
    in_specs = (P("freq", "tm"), P(), P(), P(), P(), P())
    out_specs = (P(("tm", "freq"), None, None, None), P(("tm", "freq"), None, None, None))
    return jax.shard_map(shards, mesh=mesh, in_specs=in_specs, out_specs=out_specs, check_vma=False)
```

```python
import functools
import math

import jax
import jax.numpy as jnp
import numpy as np
from jax import lax
from jax.experimental import pallas as pl
from jax.experimental.pallas import tpu as pltpu
from jax.sharding import PartitionSpec as P

INPUTS = 512
CH = 1024
L = 2048
TAPS = 16
BEAMS = 256
NTAB = 256
FR = 16
IN_DEV = 32
SLOTS = 8
BF = jnp.bfloat16
F32 = jnp.float32
MIB = 1 << 20
VM = pl.BlockSpec(memory_space=pltpu.VMEM)
SM = pl.BlockSpec(memory_space=pltpu.SMEM)
ANY = pl.BlockSpec(memory_space=pl.ANY)
HB = pl.BlockSpec(memory_space=pltpu.HBM)


def fit(fn, degree):
    nodes = np.cos(np.pi * (np.arange(64) + 0.5) / 64) * 0.125 + 0.125
    poly = np.polynomial.Chebyshev.fit(nodes, fn(np.sqrt(nodes)), degree, domain=[0.0, 0.25])
    return [float(c) for c in poly.convert(kind=np.polynomial.Polynomial).coef]


COS = fit(lambda r: np.cos(2 * np.pi * r), 6)
NEG_SIN = fit(lambda r: -np.sin(2 * np.pi * r) / r, 5)


def horner(coefs, z):
    total = z * coefs[-1] + coefs[-2]
    for c in coefs[-3::-1]:
        total = total * z + c
    return total


def cos_negsin(turns):
    r = turns - jnp.floor(turns + 0.5)
    z = r * r
    return horner(COS, z), horner(NEG_SIN, z) * r


def taps_table():
    index = np.arange(TAPS * L).astype(np.float64)
    offset = (index - TAPS * L / 2 + 0.5) / L
    window = 0.5 - 0.5 * np.cos(2.0 * np.pi * (index + 0.5) / (TAPS * L))
    return (np.sinc(offset) * window).reshape(TAPS, L).astype(np.float32)


def lane_order():
    m = np.zeros((512, 512), np.float32)
    for fl in range(4):
        for tl in range(4):
            for i in range(32):
                m[fl * 128 + tl * 32 + i, tl * 128 + fl * 32 + i] = 1
    return m


def frames_of(phase):
    return [4 + u for u in range(8)] if phase == 0 else [0, 1, 2, 3, 12, 13, 14, 15]


def frame_order():
    m = np.zeros((256, 256), np.float32)
    for c in range(2):
        for tl in range(4):
            for tm in range(8):
                for ph in range(2):
                    for th in range(2):
                        o = frames_of(ph)[th * 4 + tl]
                        t = (tm * FR + 8 + o) % 128
                        m[t * 2 + c, c * 128 + tl * 32 + tm * 4 + ph * 2 + th] = 1
    return m


def table_kernel(owner_ref, cos_ref, sin_ref, chans):
    turned = owner_ref[...].astype(F32).T
    for f in range(16):
        for t in range(8):
            column = turned[f * SLOTS : (f + 1) * SLOTS, t : t + 1]
            chans[f * 64 + t * SLOTS : f * 64 + (t + 1) * SLOTS, :] = jnp.broadcast_to(column, (SLOTS, 128))

    def group(g, carry):
        chan = chans[pl.ds(pl.multiple_of(g * 64, 64), 64), :]
        n2 = lax.broadcasted_iota(jnp.int32, (64, 128), 1).astype(F32)
        c, s = cos_negsin(chan * n2 * (1.0 / L))
        a, b = cos_negsin(chan * (128.0 / L))
        at = pl.ds(pl.multiple_of(g * 64, 64), 64)
        for n1 in range(L // 128):
            cos_ref[at, n1 * 128 : (n1 + 1) * 128] = c.astype(BF)
            sin_ref[at, n1 * 128 : (n1 + 1) * 128] = s.astype(BF)
            if n1 < L // 128 - 1:
                c, s = c * a - s * b, s * a + c * b
        return carry

    lax.fori_loop(0, 16, group, 0)


def make_table(owner_map):
    return pl.pallas_call(
        table_kernel,
        in_specs=[VM],
        out_specs=[VM, VM],
        out_shape=[pltpu.VMEM((CH, L), BF)] * 2,
        scratch_shapes=[pltpu.VMEM((CH, 128), F32)],
        cost_estimate=pl.CostEstimate(flops=16 * CH * L, transcendentals=0, bytes_accessed=8 * MIB),
        compiler_params=pltpu.CompilerParams(vmem_limit_bytes=4 * MIB),
        name="table",
    )(owner_map.reshape(8, 128))


def weight_kernel(owner_ref, beam_ref, gains_ref, delays_ref, out_ref, gain, delay):
    def pick(g, carry):
        for j in range(8):
            b = g * 8 + j
            row = beam_ref[b]
            gain[pl.ds(b, 1), :] = gains_ref[pl.ds(row, 1), :]
            delay[pl.ds(b, 1), :] = delays_ref[pl.ds(row, 1), :]
        return carry

    lax.fori_loop(0, BEAMS // 8, pick, 0)
    start = (lax.axis_index("tm") * 16 + lax.axis_index("freq")) * SLOTS

    def group(g, carry):
        s = g // (BEAMS // 64)
        at = pl.ds(pl.multiple_of(g % (BEAMS // 64) * 64, 64), 64)
        chan = owner_ref[start + s].astype(F32) * (1.0 / L)
        c, n = cos_negsin(delay[at, :] * chan)
        scaled = gain[at, :] * (1.0 / math.sqrt(INPUTS))
        out_ref[s, 0, at, :] = (scaled * c).astype(BF)
        out_ref[s, 1, at, :] = (scaled * n).astype(BF)
        return carry

    lax.fori_loop(0, SLOTS * BEAMS // 64, group, 0)


def make_weights(owner_map, beam_table, gains, delays):
    return pl.pallas_call(
        weight_kernel,
        in_specs=[SM, SM, VM, VM],
        out_specs=VM,
        out_shape=pltpu.VMEM((SLOTS, 2, BEAMS, INPUTS), BF),
        scratch_shapes=[pltpu.VMEM((BEAMS, INPUTS), F32)] * 2,
        cost_estimate=pl.CostEstimate(flops=50 * SLOTS * INPUTS * BEAMS, transcendentals=0, bytes_accessed=6 * MIB),
        compiler_params=pltpu.CompilerParams(vmem_limit_bytes=4 * MIB),
        name="weights",
    )(owner_map, beam_table, gains, delays)


def cut_kernel(firsts, source, *refs):
    outs, sem = refs[:-1], refs[-1]
    copies = [
        pltpu.make_async_copy(source.at[:, pl.ds(first * L, out.shape[1])], out, sem.at[i])
        for i, (first, out) in enumerate(zip(firsts, outs))
    ]
    for copy in copies:
        copy.start()
    for copy in copies:
        copy.wait()


def cut(voltages, ranges, name):
    return pl.pallas_call(
        functools.partial(cut_kernel, [a for a, _ in ranges]),
        in_specs=[HB],
        out_specs=[VM] * len(ranges),
        out_shape=[pltpu.VMEM((IN_DEV, (b - a) * L), BF) for a, b in ranges],
        scratch_shapes=[pltpu.SemaphoreType.DMA((len(ranges),))],
        compiler_params=pltpu.CompilerParams(vmem_limit_bytes=4 * MIB),
        cost_estimate=pl.CostEstimate(flops=0, transcendentals=0, bytes_accessed=2 * MIB),
        name=name,
    )(pltpu.with_memory_space_constraint(voltages, pltpu.HBM))


def spectra_kernel(phase, *refs):
    if phase == 0:
        own, p1, n1, taps_ref, cos_ref, sin_ref, *_, out, held, filt = refs
        p2 = n2 = None
    else:
        p2, n2, taps_ref, cos_ref, sin_ref, held, *_, out, filt = refs
        own = p1 = n1 = None
    pieces = [(p2, f) for f in range(4)] + [(p1, f) for f in range(3)] + [(own, f) for f in range(FR)]
    pieces += [(n1, f) for f in range(4)] + [(n2, f) for f in range(4)]
    now = frames_of(phase)
    later = frames_of(1)
    wanted = now + later if phase == 0 else now
    tm = lax.axis_index("tm")
    after_first = (tm != 0).astype(F32)
    before_last = (tm != lax.axis_size("tm") - 1).astype(F32)

    def column(j, carry):
        at = pl.multiple_of(j * 128, 128)
        lanes = pl.ds(at, 128)
        taps = [taps_ref[k : k + 1, lanes] for k in range(TAPS)]
        for g in range(IN_DEV // 16):
            rows = lambda o, among: slice(among.index(o) * IN_DEV + g * 16, among.index(o) * IN_DEV + g * 16 + 16)
            acc = {}
            for f, (ref, i) in enumerate(pieces):
                if f == 7:
                    for o in acc:
                        acc[o] = acc[o] * after_first
                    if phase == 1:
                        for o in now:
                            held_o = held[rows(o, later), lanes]
                            acc[o] = acc[o] + held_o if o in acc else held_o
                if f == 23 and phase == 0:
                    for o in acc:
                        if o >= 8:
                            acc[o] = acc[o] * before_last
                hit = [o for o in wanted if o <= f < o + TAPS]
                if ref is not None and hit:
                    x = ref[g * 16 : g * 16 + 16, pl.ds(i * L + at, 128)].astype(F32)
                    for o in hit:
                        term = taps[f - o] * x
                        acc[o] = acc[o] + term if o in acc else term
                for o in hit:
                    if o == f - TAPS + 1 and o in now:
                        filt[rows(o, now), lanes] = acc.pop(o).astype(BF)
                    elif o in later and phase == 0 and f == min(o + TAPS - 1, 26):
                        held[rows(o, later), lanes] = acc.pop(o)
        return carry

    lax.fori_loop(0, L // 128, column, 0)
    for q in range(1):
        rows = slice(q * 1024, q * 1024 + 1024)
        dot = lambda ref: lax.dot_general(
            ref[rows, :], filt[...], (((1,), (1,)), ((), ())), preferred_element_type=F32
        ) * (1.0 / math.sqrt(L))
        re, im = dot(cos_ref), dot(sin_ref)
        for th in range(2):
            lanes = slice(th * 128, th * 128 + 128)
            both = [re[:, lanes].reshape(128, SLOTS, 128), im[:, lanes].reshape(128, SLOTS, 128)]
            at = phase * 32 + th * 16
            out[q * 128 : q * 128 + 128, at : at + 16, :] = jnp.concatenate(both, 1).astype(BF)


def make_spectra(phase, args, after=()):
    ready = len(args)
    args = [*args, *after]
    out = pltpu.VMEM((128, 64, 128), BF)
    return pl.pallas_call(
        functools.partial(spectra_kernel, phase),
        in_specs=[VM] * ready + [VM if phase else ANY] * len(after),
        out_specs=VM if phase else [VM, VM],
        out_shape=out if phase else [out, pltpu.VMEM((8 * IN_DEV, L), F32)],
        input_output_aliases={len(args) - 1: 0} if phase else {},
        scratch_shapes=[pltpu.VMEM((8 * IN_DEV, L), BF)],
        compiler_params=pltpu.CompilerParams(vmem_limit_bytes=8 * MIB),
        cost_estimate=pl.CostEstimate(flops=4 * CH * L * 256, transcendentals=0, bytes_accessed=12 * MIB),
        name="spectra%d" % phase,
    )(*args)


def pair_kernel(
    flag_ref, twice_ref, lanes_ref, frames_ref, got_ref, weight_ref, vis, beam, y, vis_buf, beam_buf, sem, beam_sem
):
    dot = functools.partial(jnp.dot, preferred_element_type=F32)
    dot_t = lambda a, b: lax.dot_general(a, b, (((1,), (1,)), ((), ())), preferred_element_type=F32)
    used = jnp.broadcast_to(flag_ref[...].astype(F32), (8, INPUTS // 2)).astype(BF)
    flags = dot(used, twice_ref[...])[0:1]
    for fh in range(4):
        parts = [got_ref[(fh * 4 + fl) * 8 : (fh * 4 + fl) * 8 + 8].reshape(512, 128) for fl in range(4)]
        block = dot(jnp.concatenate(parts, 1), lanes_ref[...])
        flag = flags[:, fh * 128 : (fh + 1) * 128]
        for tl in range(4):
            y[fh * 4 + tl] = block[:, tl * 128 : (tl + 1) * 128] * flag
    def prepare(s):
        rows = [pl.ds(r * 8 + s, 32, stride=16) for r in range(2)]
        pieces = [[[y[fh * 4 + tl, at, :] for fh in range(4)] for tl in range(4)] for at in rows]
        w = jnp.concatenate([jnp.concatenate([jnp.concatenate(p, 1) for p in half], 0) for half in pieces], 0).astype(BF)
        return w, w.T

    def finish(s, by):
        b_re = by[:BEAMS, :128] - by[BEAMS:, 128:]
        b_im = by[BEAMS:, :128] + by[:BEAMS, 128:]
        both = jnp.concatenate([b_re, b_im], 1).astype(BF)
        beam_buf[s] = dot_t(frames_ref[...], both).astype(BF).reshape(128, 2, BEAMS)
        copy = pltpu.make_async_copy(beam_buf.at[s], beam.at[s], beam_sem.at[s])
        copy.start()
        return copy

    copies = []
    for s in range(SLOTS):
        w, wt = prepare(s)
        by = dot(weight_ref[s].reshape(2 * BEAMS, INPUTS), wt)
        vt = jnp.concatenate([wt[:, 128:], -wt[:, :128]], 1)
        for c, left in enumerate((wt, vt)):
            vis_buf[s, c] = (dot(left, w) * (1.0 / 128)).astype(BF)
            copies.append(pltpu.make_async_copy(vis_buf.at[s, c], vis.at[s, c], sem.at[s, c]))
            copies[-1].start()
        copies.append(finish(s, by))
    for copy in copies:
        copy.wait()


def make_outputs(flags, got, weights):
    twice = np.repeat(np.eye(INPUTS // 2), 2, 1)
    consts = [jnp.asarray(m, BF) for m in (twice, lane_order(), frame_order())]
    return pl.pallas_call(
        pair_kernel,
        in_specs=[VM] * 6,
        out_specs=[ANY, ANY],
        out_shape=[
            jax.ShapeDtypeStruct((SLOTS, 2, INPUTS, INPUTS), BF),
            jax.ShapeDtypeStruct((SLOTS, 128, 2, BEAMS), BF),
        ],
        scratch_shapes=[
            pltpu.VMEM((16, 512, 128), F32),
            pltpu.VMEM((SLOTS, 2, INPUTS, INPUTS), BF),
            pltpu.VMEM((SLOTS, 128, 2, BEAMS), BF),
            pltpu.SemaphoreType.DMA((SLOTS, 2)),
            pltpu.SemaphoreType.DMA((SLOTS,)),
        ],
        compiler_params=pltpu.CompilerParams(vmem_limit_bytes=20 * MIB),
        cost_estimate=pl.CostEstimate(flops=5_000_000_000, transcendentals=0, bytes_accessed=16 * MIB),
        name="pairs",
    )(flags, *consts, got, weights)


def shards(voltages, station_flags, owner_map, beam_table, table_gains, table_delays):
    n_time = lax.axis_size("tm")
    up = lambda x: lax.ppermute(x, "tm", [(i, (i + 1) % n_time) for i in range(n_time)])
    down = lambda x: lax.ppermute(x, "tm", [(i, (i - 1) % n_time) for i in range(n_time)])
    down0, up0, down1, up1 = cut(voltages, [(0, 4), (13, 16), (4, 8), (9, 13)], "cut")
    n1, p1 = down(down0), up(up0)
    n2, p2 = down(down1), up(up1)
    cos, sin = make_table(owner_map)
    taps = jnp.asarray(taps_table())
    weights = make_weights(owner_map, beam_table, table_gains, table_delays)
    flags = station_flags.reshape(1, INPUTS // 2)
    first, held = make_spectra(0, (voltages, p1, n1, taps, cos, sin), (weights,))
    spectra = make_spectra(1, (p2, n2, taps, cos, sin, held), (first,))
    got = lax.all_to_all(spectra, ("freq", "tm"), split_axis=0, concat_axis=0, tiled=True)
    return make_outputs(flags, got, weights)


def solution(mesh):
    in_specs = (P("freq", "tm"), P(), P(), P(), P(), P())
    out_specs = (P(("tm", "freq"), None, None, None), P(("tm", "freq"), None, None, None))
    return jax.shard_map(shards, mesh=mesh, in_specs=in_specs, out_specs=out_specs, check_vma=False)
```
